32 devices in a mesh: query: 2 (over core), key: 2 (over x), heads: 8 (over z, y).
Axes of the slice: x: 2, y: 2, z: 4, core: 2. Of those that a mesh axis runs over, the one named last changes fastest.
Arguments:
- pair_feats: bfloat16 [1024, 64, 2048], P(('query', 'heads'), None, 'key'), may hold values from -6 to 6
- bucket_ids: int32 [1024, 2048], P(('query', 'heads'), 'key'), may hold values from 0 to 31
- ln_gain: float32 [64], replicated, may hold values from 0.5 to 1.5
- w_in: bfloat16 [64, 256], replicated, may hold values from -0.75 to 0.75
- b_in: float32 [256], replicated, may hold values from -3 to 3
- w_out: bfloat16 [256, 8], replicated, may hold values from -0.375 to 0.375
- bucket_table: bfloat16 [32, 8], replicated, may hold values from -4 to 4
- key_mask: int32 [2048], P('key'), may hold values 0 or 1
- q_heads: bfloat16 [8, 32, 1024], P('heads', None, 'query'), may hold values from -6 to 6
- k_heads: bfloat16 [8, 32, 2048], P('heads', None, 'key'), may hold values from -6 to 6
- v_heads: bfloat16 [8, 32, 2048], P('heads', None, 'key'), may hold values from -6 to 6
- out_heads: bfloat16 [8, 32, 1024], P('heads', None, 'query'), may hold values from -6 to 6
- dout_heads: bfloat16 [8, 32, 1024], P('heads', None, 'query'), may hold values from -96 to 96
- log_norm: float32 [8, 1024], P('heads', 'query'), may hold values from 8 to 10
Outputs:
- grad_pairs: bfloat16 [1024, 64, 2048], P(('query', 'heads'), None, 'key')
- grad_q: bfloat16 [8, 32, 1024], P('heads', None, 'query')
- grad_k: bfloat16 [8, 32, 2048], P('heads', None, 'key')
- grad_v: bfloat16 [8, 32, 2048], P('heads', None, 'key')
The draws below stay inside these ranges and needn't reach their ends.
All inputs are finite; a program needn't handle non-finite values. No bound on the sum of `key_mask` on one device may be relied on, other than what follows from the above.
Results may differ from the reference program's by a relative error of at most 0.012.
The reference program's roundings to bfloat16 on the way (of `normed`, `hidden`, `bias_vals`, `probs_low`, `dscores` and `dpre`) count: a program that leaves them out, or rounds other values in their place, can miss the bound.
Values may be sent and summed in bfloat16 or wider, within the bound.
No kernel may reach another device: no remote copies, remote signals or barrier semaphores. Data moves between devices by JAX's collectives and lax.ppermute only.
A program may use at most 128 MiB of HBM per device.

```python
import math
import jax
import jax.numpy as jnp
from jax import lax

C = 64
HID = 256
H = 8
DH = 32
BUCKETS = 32
NQ = 1024
NK = 2048


def place_ends(result, own_key, smallest, high):
    place = [jax.random.randint(jax.random.fold_in(own_key, axis), (), 0, length) for axis, length in enumerate(result.shape)]
    widest = result.shape.index(max(result.shape))
    next_to = place[:widest] + [(place[widest] + 1) % result.shape[widest]] + place[widest + 1:]
    return result.at[tuple(place)].set(smallest).at[tuple(next_to)].set(high)


def level_of(rng, extent, split, low, largest):
    def one(axis_at, parts):
        steps = jax.random.uniform(jax.random.fold_in(jax.random.fold_in(rng, 6), axis_at), (parts,), jnp.float32, low / len(split), largest / len(split))
        return jnp.repeat(jnp.exp(steps), extent[axis_at] // parts).reshape((-1,) + (1,) * (len(extent) - axis_at - 1))

    level = one(*split[0])
    for cut in split[1:]:
        level = level * one(*cut)
    return level


def normal_values(own_key, extent, scale, reach, cuts=(), held_as=jnp.bfloat16):
    loudness = level_of(own_key, extent, cuts, -0.22, 0.18) if cuts else 1.0
    result = jax.random.normal(own_key, extent, jnp.float32) * scale * loudness
    return jnp.minimum(jnp.maximum(result, -reach), reach).astype(held_as)


def setup_inputs(seed: int = 0) -> dict:
    keys = jax.random.split(jax.random.key(seed), 15)
    pair_feats = normal_values(keys[0], (NQ, C, NK), 1.0, 6.0, ((0, 16), (2, 2)))
    bucket_ids = place_ends(jax.random.randint(keys[1], (NQ, NK), 0, BUCKETS), jax.random.fold_in(keys[1], 1), 0, BUCKETS - 1).astype(jnp.int32)
    ln_gain = jnp.clip(1.0 + 0.1 * jax.random.normal(keys[2], (C,), jnp.float32), 0.5, 1.5)
    w_in = normal_values(keys[3], (C, HID), C ** -0.5, 0.75)
    b_in = normal_values(keys[4], (HID,), 0.5, 3.0, (), jnp.float32)
    w_out = normal_values(keys[5], (HID, H), HID ** -0.5, 0.375)
    bucket_table = normal_values(keys[6], (BUCKETS, H), 1.0, 4.0)
    key_mask = place_ends((jax.random.randint(keys[7], (NK,), 0, 8) < 7).astype(jnp.int32), jax.random.fold_in(keys[7], 1), 0, 1)
    q_heads = normal_values(keys[8], (H, DH, NQ), 1.0, 6.0, ((0, 8), (2, 2)))
    k_heads = normal_values(keys[9], (H, DH, NK), 1.0, 6.0, ((0, 8), (2, 2)))
    v_heads = normal_values(keys[10], (H, DH, NK), 1.0, 6.0, ((0, 8), (2, 2)))
    out_heads = normal_values(keys[11], (H, DH, NQ), 1.0, 6.0, ((0, 8), (2, 2)))
    dout_heads = normal_values(keys[12], (H, DH, NQ), 16.0, 96.0, ((0, 8), (2, 2)))
    log_norm = jnp.clip(8.0 + 2.0 * jax.random.uniform(keys[13], (H, NQ), jnp.float32) ** level_of(keys[13], (H, NQ), ((0, 8), (1, 2)), -0.2, 0.2), 8.0, 10.0)
    return {"pair_feats": pair_feats, "bucket_ids": bucket_ids, "ln_gain": ln_gain, "w_in": w_in, "b_in": b_in, "w_out": w_out, "bucket_table": bucket_table, "key_mask": key_mask, "q_heads": q_heads, "k_heads": k_heads, "v_heads": v_heads, "out_heads": out_heads, "dout_heads": dout_heads, "log_norm": log_norm}


def gelu_parts(pre_act):
    cdf_val = 0.5 * (1.0 + jax.scipy.special.erf(pre_act * (1.0 / math.sqrt(2.0))))
    density = jnp.exp(-0.5 * pre_act * pre_act) * (1.0 / math.sqrt(2.0 * math.pi))
    return (pre_act * cdf_val, cdf_val + pre_act * density)

def normalize(pair_blk, ln_gain):
    values = pair_blk.astype(jnp.float32)
    centre = values - lax.optimization_barrier(jnp.mean(values, axis=1, keepdims=True))
    inv_std = lax.rsqrt(lax.optimization_barrier(jnp.mean(centre * centre, axis=1, keepdims=True)) + 1e-05)
    unit_pairs = centre * inv_std
    normed = (unit_pairs * ln_gain[None, :, None]).astype(jnp.bfloat16)
    return (unit_pairs, inv_std, normed)

def make_bias(pair_blk, bucket_blk, ln_gain, w_in, b_in, w_out, bucket_table):
    unit_pairs, inv_std, normed = normalize(pair_blk, ln_gain)
    pre_act = jnp.einsum('rck,cf->rfk', normed.astype(jnp.float32), w_in.astype(jnp.float32)) + b_in[None, :, None]
    gelu_val, gelu_slope = gelu_parts(pre_act)
    hidden = gelu_val.astype(jnp.bfloat16)
    lookup = jnp.transpose(bucket_table[bucket_blk].astype(jnp.float32), (0, 2, 1))
    mixed = jnp.einsum('rfk,fh->rhk', hidden.astype(jnp.float32), w_out.astype(jnp.float32))
    return (mixed + lookup).astype(jnp.bfloat16)

def pair_grad(pair_blk, ln_gain, w_in, b_in, w_out, dscores):
    unit_pairs, inv_std, normed = normalize(pair_blk, ln_gain)
    pre_act = jnp.einsum('rck,cf->rfk', normed.astype(jnp.float32), w_in.astype(jnp.float32)) + b_in[None, :, None]
    gelu_val, gelu_slope = gelu_parts(pre_act)
    dhidden = jnp.einsum('rhk,fh->rfk', dscores.astype(jnp.float32), w_out.astype(jnp.float32))
    dpre = (dhidden * gelu_slope).astype(jnp.bfloat16)
    dunit = jnp.einsum('rfk,cf->rck', dpre.astype(jnp.float32), w_in.astype(jnp.float32)) * ln_gain[None, :, None]
    first_mean = lax.optimization_barrier(jnp.mean(dunit, axis=1, keepdims=True))
    second_mean = lax.optimization_barrier(jnp.mean(dunit * unit_pairs, axis=1, keepdims=True))
    return (inv_std * (dunit - first_mean - unit_pairs * second_mean)).astype(jnp.bfloat16)

def reference(pair_feats, bucket_ids, ln_gain, w_in, b_in, w_out, bucket_table, key_mask, q_heads, k_heads, v_heads, out_heads, dout_heads, log_norm):
    rows_per = math.gcd(NQ, 16)
    score_scale = 1.0 / math.sqrt(DH)
    key_live = (key_mask == 1)[None, None, :]
    keys_f32 = k_heads.astype(jnp.float32)
    values_f32 = v_heads.astype(jnp.float32)

    def row_step(running, counter):
        dk_acc, dv_acc = running
        begin_row = (counter * rows_per).astype(jnp.int32)
        pair_blk = lax.dynamic_slice_in_dim(pair_feats, begin_row, rows_per, 0)
        bucket_blk = lax.dynamic_slice_in_dim(bucket_ids, begin_row, rows_per, 0)
        q_blk = lax.dynamic_slice_in_dim(q_heads, begin_row, rows_per, 2).astype(jnp.float32)
        out_blk = lax.dynamic_slice_in_dim(out_heads, begin_row, rows_per, 2).astype(jnp.float32)
        dout_blk = lax.dynamic_slice_in_dim(dout_heads, begin_row, rows_per, 2).astype(jnp.float32)
        norm_blk = lax.dynamic_slice_in_dim(log_norm, begin_row, rows_per, 1)
        bias_vals = make_bias(pair_blk, bucket_blk, ln_gain, w_in, b_in, w_out, bucket_table)
        scores = jnp.einsum('hdi,hdj->hij', q_blk, keys_f32) * score_scale + jnp.transpose(bias_vals.astype(jnp.float32), (1, 0, 2))
        attn_probs = jnp.where(key_live, jnp.exp(scores - norm_blk[:, :, None]), 0.0)
        probs_low = attn_probs.astype(jnp.bfloat16)
        deltas = lax.optimization_barrier(jnp.sum(dout_blk * out_blk, axis=1))
        dprobs = jnp.einsum('hdi,hdj->hij', dout_blk, values_f32)
        dscores = (attn_probs * (dprobs - deltas[:, :, None])).astype(jnp.bfloat16)
        dscore_f = dscores.astype(jnp.float32)
        dv_acc = dv_acc + jnp.einsum('hdi,hij->hdj', dout_blk, probs_low.astype(jnp.float32))
        dk_acc = dk_acc + jnp.einsum('hdi,hij->hdj', q_blk, dscore_f)
        dq_blk = (jnp.einsum('hdj,hij->hdi', keys_f32, dscore_f) * score_scale).astype(jnp.bfloat16)
        grad_blk = pair_grad(pair_blk, ln_gain, w_in, b_in, w_out, jnp.transpose(dscores, (1, 0, 2)))
        return ((dk_acc, dv_acc), (dq_blk, grad_blk))
    zero_grad = jnp.zeros((H, DH, NK), jnp.float32)
    block_ids = jnp.arange(NQ // rows_per, dtype=jnp.int32)
    (dk_acc, dv_acc), (dq_blocks, grad_blocks) = lax.scan(row_step, (zero_grad, zero_grad), block_ids)
    grad_q = jnp.transpose(dq_blocks, (1, 2, 0, 3)).reshape(H, DH, NQ)
    grad_pairs = grad_blocks.reshape(NQ, C, NK)
    grad_k = (dk_acc * score_scale).astype(jnp.bfloat16)
    grad_v = dv_acc.astype(jnp.bfloat16)
    return (grad_pairs, grad_q, grad_k, grad_v)
```

```python
import functools
import math

import jax
import jax.numpy as jnp
from jax import lax
from jax.experimental import pallas as pl
from jax.experimental.pallas import tpu as pltpu
from jax.sharding import PartitionSpec as P

F32 = jnp.float32
BF16 = jnp.bfloat16
RSQRT2 = 1.0 / math.sqrt(2.0)
EXP2_SCALE = -0.5 / math.log(2.0)
EXP2_SHIFT = math.log2(2.0 / math.sqrt(2.0 * math.pi))
PAD = 16
VMEM_LIMIT = 60 << 20


def full_spec(array):
    return pl.BlockSpec(array.shape, lambda *_: (0,) * array.ndim)


def divisor(total, largest):
    return math.gcd(total, largest)


def split_three(values):
    high = lax.reduce_precision(values, 8, 7)
    mid = lax.reduce_precision(values - high, 8, 7)
    low = lax.reduce_precision(values - high - mid, 8, 7)
    return [piece.astype(BF16) for piece in (high, mid, low)]


def axis_sum(values, name):
    if lax.axis_size(name) == 2:
        return values + lax.ppermute(values, name, [(0, 1), (1, 0)])
    return lax.psum(values, name)


def unit_norm(values):
    centre = values - jnp.mean(values, axis=0, keepdims=True)
    inv_std = lax.rsqrt(jnp.mean(centre * centre, axis=0, keepdims=True) + 1e-05)
    return centre * inv_std, inv_std


def forward_kernel(
    pair_ref, bucket_ref, w_pre_ref, w_mix_ref, table_ref, gain_ref, slope_ref, bias_ref, *, group, tile
):
    rows, chans, keys = pair_ref.shape
    heads = w_mix_ref.shape[0]
    extra = w_pre_ref.shape[1] - chans
    buckets = table_ref.shape[1]
    key_tiles = keys // tile
    ones = jnp.where(lax.broadcasted_iota(jnp.int32, (extra, tile), 0) < 3, 1.0, 0.0).astype(BF16)

    def one_row(row, cols):
        unit_pairs, _ = unit_norm(pair_ref[row, :, cols].astype(F32))
        normed = (unit_pairs * gain_ref[...]).astype(BF16)
        pre_act = jnp.dot(
            w_pre_ref[...], jnp.concatenate([normed, ones], axis=0), preferred_element_type=F32
        )
        cdf2 = lax.erf(pre_act * RSQRT2) + 1.0
        hidden2 = (pre_act * cdf2).astype(BF16)
        density2 = jnp.exp2(pre_act * pre_act * EXP2_SCALE + EXP2_SHIFT)
        slope_ref[row, :, cols] = (cdf2 + pre_act * density2).astype(BF16)
        bucket_iota = lax.broadcasted_iota(jnp.int32, (buckets, tile), 0)
        onehot = jnp.where(bucket_ref[row, :, cols] == bucket_iota, 1.0, 0.0).astype(BF16)
        mixed = jnp.dot(w_mix_ref[...], hidden2, preferred_element_type=F32)
        return mixed + jnp.dot(table_ref[...], onehot, preferred_element_type=F32)

    def step(index, carry):
        row_group = index // key_tiles
        cols = pl.ds(pl.multiple_of((index % key_tiles) * tile, tile), tile)
        outs = [one_row(row_group * group + member, cols) for member in range(group)]
        size = group * heads
        bias_ref[pl.ds(pl.multiple_of(row_group * size, size), size), cols] = jnp.concatenate(
            outs, axis=0
        ).astype(BF16)
        return carry

    lax.fori_loop(0, (rows // group) * key_tiles, step, 0)


def forward_call(pair_feats, bucket_ids, w_pre, w_mix, table, gain):
    rows, chans, keys = pair_feats.shape
    hid = w_pre.shape[0]
    heads = w_mix.shape[0]
    block = divisor(rows, 4)
    group = divisor(block, 4)
    tile = divisor(keys, 512)
    return pl.pallas_call(
        functools.partial(forward_kernel, group=group, tile=tile),
        grid=(rows // block,),
        in_specs=[
            pl.BlockSpec((block, chans, keys), lambda i: (i, 0, 0)),
            pl.BlockSpec((block, 1, keys), lambda i: (i, 0, 0)),
            full_spec(w_pre),
            full_spec(w_mix),
            full_spec(table),
            full_spec(gain),
        ],
        out_specs=[
            pl.BlockSpec((block, hid, keys), lambda i: (i, 0, 0)),
            pl.BlockSpec((block * heads, keys), lambda i: (i, 0)),
        ],
        out_shape=[
            jax.ShapeDtypeStruct((rows, hid, keys), BF16),
            jax.ShapeDtypeStruct((rows * heads, keys), BF16),
        ],
        compiler_params=pltpu.CompilerParams(vmem_limit_bytes=VMEM_LIMIT),
        cost_estimate=pl.CostEstimate(
            flops=2 * rows * keys * hid * 256,
            bytes_accessed=2 * rows * keys * (hid + chans),
            transcendentals=2 * rows * keys * hid,
        ),
        name="pair_forward",
    )(pair_feats, bucket_ids[:, None, :], w_pre, w_mix, table, gain)


def attention_kernel(
    bias_ref, kv_ref, qd_ref, mask_ref, ds_ref, dkv_ref, dq_ref, q_rows, d_rows, q_cols, d_cols, norm_ref,
    delta_ref, dq_acc, *, head_dim
):
    heads, _, rows = qd_ref.shape
    tile = bias_ref.shape[1]
    width = heads * head_dim
    flat = rows * heads
    scale = 1.0 / math.sqrt(head_dim)
    nt = (((1,), (1,)), ((), ()))
    step = pl.program_id(0)
    expand = (
        lax.broadcasted_iota(jnp.int32, (flat, rows), 0) // heads
        == lax.broadcasted_iota(jnp.int32, (flat, rows), 1)
    )

    @pl.when(step == 0)
    def _():
        expand_low = jnp.where(expand, 1.0, 0.0).astype(BF16)
        own_rows = (
            lax.broadcasted_iota(jnp.int32, (flat, width), 0) % heads
            == lax.broadcasted_iota(jnp.int32, (flat, width), 1) // head_dim
        )
        own_cols = (
            lax.broadcasted_iota(jnp.int32, (width, flat), 1) % heads
            == lax.broadcasted_iota(jnp.int32, (width, flat), 0) // head_dim
        )
        for begin, by_rows, by_cols in ((0, q_rows, q_cols), (head_dim, d_rows, d_cols)):
            block = qd_ref[:, begin : begin + head_dim, :].reshape(width, rows)
            spread = lax.dot_general(expand_low, block, nt, preferred_element_type=F32)
            by_rows[...] = jnp.where(own_rows, spread, 0.0).astype(BF16)
            spread = lax.dot_general(block, expand_low, nt, preferred_element_type=F32)
            by_cols[...] = jnp.where(own_cols, spread, 0.0).astype(BF16)
        tail = qd_ref[:, 2 * head_dim :, :].astype(F32)
        lane = lax.broadcasted_iota(jnp.int32, (rows, heads, rows), 2)
        own_lane = lane == lax.broadcasted_iota(jnp.int32, (rows, heads, rows), 0)
        for begin, target in ((0, norm_ref), (3, delta_ref)):
            pieces = tail[:, begin, :] + tail[:, begin + 1, :] + tail[:, begin + 2, :]
            column = jnp.sum(jnp.where(own_lane, pieces[None], 0.0), axis=2, keepdims=True)
            target[...] = jnp.broadcast_to(column.reshape(flat, 1), target.shape)
        dq_acc[...] = jnp.zeros_like(dq_acc)

    copies = tile // norm_ref.shape[1]
    norm = jnp.concatenate([norm_ref[...]] * copies, axis=1)
    delta = jnp.concatenate([delta_ref[...]] * copies, axis=1)
    keys = kv_ref[:, :head_dim, :].reshape(width, tile)
    values = kv_ref[:, head_dim:, :].reshape(width, tile)
    scores = jnp.dot(q_rows[...], keys, preferred_element_type=F32) * scale + bias_ref[...].astype(F32)
    probs = jnp.where(mask_ref[...] == 1, jnp.exp(scores - norm), 0.0)
    dprobs = jnp.dot(d_rows[...], values, preferred_element_type=F32)
    dscores = (probs * (dprobs - delta)).astype(BF16)
    ds_ref[...] = dscores
    dk_part = jnp.dot(q_cols[...], dscores, preferred_element_type=F32)
    dv_part = jnp.dot(d_cols[...], probs.astype(BF16), preferred_element_type=F32)
    dkv_ref[:, :head_dim, :] = dk_part.reshape(heads, head_dim, tile).astype(dkv_ref.dtype)
    dkv_ref[:, head_dim:, :] = dv_part.reshape(heads, head_dim, tile).astype(dkv_ref.dtype)
    dq_acc[...] += lax.dot_general(keys, dscores, nt, preferred_element_type=F32)

    @pl.when(step == pl.num_programs(0) - 1)
    def _():
        own_cols = (
            lax.broadcasted_iota(jnp.int32, (width, flat), 1) % heads
            == lax.broadcasted_iota(jnp.int32, (width, flat), 0) // head_dim
        )
        mine = jnp.where(own_cols, dq_acc[...], 0.0)
        total = jnp.dot(
            mine, jnp.where(expand, 1.0, 0.0), precision=lax.Precision.HIGHEST, preferred_element_type=F32
        )
        dq_ref[...] = total.reshape(heads, head_dim, rows)


def attention_call(bias, kv, qd, key_mask, head_dim):
    flat, keys = bias.shape
    heads, depth, rows = qd.shape
    width = heads * head_dim
    tile = divisor(keys, 256)
    lanes = divisor(tile, 128)
    return pl.pallas_call(
        functools.partial(attention_kernel, head_dim=head_dim),
        grid=(keys // tile,),
        in_specs=[
            pl.BlockSpec((flat, tile), lambda i: (0, i)),
            pl.BlockSpec((heads, 2 * head_dim, tile), lambda i: (0, 0, i)),
            full_spec(qd),
            pl.BlockSpec((1, tile), lambda i: (0, i)),
        ],
        out_specs=[
            pl.BlockSpec((flat, tile), lambda i: (0, i)),
            pl.BlockSpec((heads, 2 * head_dim, tile), lambda i: (0, 0, i)),
            pl.BlockSpec((heads, head_dim, rows), lambda i: (0, 0, 0)),
        ],
        out_shape=[
            jax.ShapeDtypeStruct((flat, keys), BF16),
            jax.ShapeDtypeStruct((heads, 2 * head_dim, keys), BF16),
            jax.ShapeDtypeStruct((heads, head_dim, rows), F32),
        ],
        scratch_shapes=[
            pltpu.VMEM((flat, width), BF16),
            pltpu.VMEM((flat, width), BF16),
            pltpu.VMEM((width, flat), BF16),
            pltpu.VMEM((width, flat), BF16),
            pltpu.VMEM((flat, lanes), F32),
            pltpu.VMEM((flat, lanes), F32),
            pltpu.VMEM((width, flat), F32),
        ],
        compiler_params=pltpu.CompilerParams(vmem_limit_bytes=VMEM_LIMIT),
        cost_estimate=pl.CostEstimate(
            flops=10 * flat * keys * width, bytes_accessed=8 * flat * keys, transcendentals=flat * keys
        ),
        name="pair_attention",
    )(bias, kv, qd, key_mask.reshape(1, keys))


def backward_kernel(pair_ref, ds_ref, slope_ref, w_back_ref, w_in_ref, gain_ref, out_ref, *, group, tile):
    rows, chans, keys = pair_ref.shape
    heads = w_back_ref.shape[1]
    key_tiles = keys // tile

    def step(index, carry):
        row_group = index // key_tiles
        cols = pl.ds(pl.multiple_of((index % key_tiles) * tile, tile), tile)
        size = group * heads
        dscores = ds_ref[pl.ds(pl.multiple_of(row_group * size, size), size), cols]
        for member in range(group):
            row = row_group * group + member
            unit_pairs, inv_std = unit_norm(pair_ref[row, :, cols].astype(F32))
            dhidden = jnp.dot(
                w_back_ref[...], dscores[member * heads : (member + 1) * heads], preferred_element_type=F32
            )
            dpre = (dhidden * slope_ref[row, :, cols].astype(F32)).astype(BF16)
            dunit = jnp.dot(w_in_ref[...], dpre, preferred_element_type=F32) * gain_ref[...]
            first_mean = jnp.mean(dunit, axis=0, keepdims=True)
            second_mean = jnp.mean(dunit * unit_pairs, axis=0, keepdims=True)
            grad = inv_std * (dunit - first_mean - unit_pairs * second_mean)
            out_ref[row, :, cols] = grad.astype(BF16)
        return carry

    lax.fori_loop(0, (rows // group) * key_tiles, step, 0)


def backward_call(pair_feats, dscores, slope, w_back, w_in, gain):
    rows, chans, keys = pair_feats.shape
    hid, heads = w_back.shape
    block = divisor(rows, 4)
    group = divisor(block, 4)
    tile = divisor(keys, 512)
    return pl.pallas_call(
        functools.partial(backward_kernel, group=group, tile=tile),
        grid=(rows // block,),
        in_specs=[
            pl.BlockSpec((block, chans, keys), lambda i: (i, 0, 0)),
            pl.BlockSpec((block * heads, keys), lambda i: (i, 0)),
            pl.BlockSpec((block, hid, keys), lambda i: (i, 0, 0)),
            full_spec(w_back),
            full_spec(w_in),
            full_spec(gain),
        ],
        out_specs=pl.BlockSpec((block, chans, keys), lambda i: (i, 0, 0)),
        out_shape=jax.ShapeDtypeStruct((rows, chans, keys), BF16),
        compiler_params=pltpu.CompilerParams(vmem_limit_bytes=VMEM_LIMIT),
        cost_estimate=pl.CostEstimate(
            flops=2 * rows * keys * hid * 256,
            bytes_accessed=2 * rows * keys * (hid + 2 * chans),
            transcendentals=0,
        ),
        name="pair_backward",
    )(pair_feats, dscores, slope, w_back, w_in, gain)


def per_device(
    pair_feats,
    bucket_ids,
    ln_gain,
    w_in,
    b_in,
    w_out,
    bucket_table,
    key_mask,
    q_heads,
    k_heads,
    v_heads,
    out_heads,
    dout_heads,
    log_norm,
):
    axis_size = lax.axis_size("heads")
    own_heads, head_dim, queries = q_heads.shape
    keys = k_heads.shape[2]
    score_scale = 1.0 / math.sqrt(head_dim)

    kv = jnp.concatenate([k_heads, v_heads], axis=1)
    kv_all = lax.all_to_all(
        jnp.broadcast_to(kv[None], (axis_size,) + kv.shape), "heads", split_axis=0, concat_axis=0, tiled=True
    ).reshape(axis_size * own_heads, 2 * head_dim, keys)
    deltas = jnp.sum(dout_heads.astype(F32) * out_heads.astype(F32), axis=1)
    scalars = [piece[:, None, :] for piece in split_three(log_norm) + split_three(deltas)]
    fill = -(2 * head_dim + len(scalars)) % PAD
    packed = jnp.concatenate(
        [q_heads, dout_heads] + scalars + [jnp.zeros((own_heads, fill, queries), BF16)], axis=1
    )
    qd_all = lax.all_to_all(packed, "heads", split_axis=2, concat_axis=0, tiled=True)

    gain = ln_gain[:, None]
    bias_rows = [piece[:, None] for piece in split_three(b_in)]
    hid = b_in.shape[0]
    w_pre = jnp.concatenate([w_in.T] + bias_rows + [jnp.zeros((hid, PAD - 3), BF16)], axis=1)
    half_out = w_out * jnp.asarray(0.5, BF16)

    slope, bias_vals = forward_call(pair_feats, bucket_ids, w_pre, half_out.T, bucket_table.T, gain)
    dscores, dkv_part, dq_part = attention_call(bias_vals, kv_all, qd_all, key_mask, head_dim)
    dkv_all = lax.all_to_all(dkv_part, "heads", split_axis=0, concat_axis=0, tiled=True)
    dq_all = lax.all_to_all(dq_part, "heads", split_axis=0, concat_axis=2, tiled=True)
    grad_pairs = backward_call(pair_feats, dscores, slope, half_out, w_in, gain)

    dkv_sum = jnp.sum(
        dkv_all.reshape(axis_size, own_heads, 2 * head_dim, keys).astype(F32), axis=0
    )
    dkv_sum = axis_sum(dkv_sum, "query")
    dq_sum = axis_sum(dq_all, "key")
    grad_q = (dq_sum * score_scale).astype(BF16)
    grad_k = (dkv_sum[:, :head_dim] * score_scale).astype(BF16)
    grad_v = dkv_sum[:, head_dim:].astype(BF16)
    return (grad_pairs, grad_q, grad_k, grad_v)


def solution(mesh):
    def traced(*args):
        with jax.sharding.use_abstract_mesh(mesh.abstract_mesh):
            return jax.shard_map(
                per_device,
                mesh=mesh,
                in_specs=(
                    P(("query", "heads"), None, "key"),
                    P(("query", "heads"), "key"),
                    P(),
                    P(),
                    P(),
                    P(),
                    P(),
                    P("key"),
                    P("heads", None, "query"),
                    P("heads", None, "key"),
                    P("heads", None, "key"),
                    P("heads", None, "query"),
                    P("heads", None, "query"),
                    P("heads", "query"),
                ),
                out_specs=(
                    P(("query", "heads"), None, "key"),
                    P("heads", None, "query"),
                    P("heads", None, "key"),
                    P("heads", None, "key"),
                ),
                check_vma=False,
            )(*args)

    return traced
```

```python
import functools
import math

import jax
import jax.numpy as jnp
from jax import lax
from jax.experimental import pallas as pl
from jax.experimental.pallas import tpu as pltpu
from jax.sharding import PartitionSpec as P

F32 = jnp.float32
BF16 = jnp.bfloat16
RSQRT2 = 1.0 / math.sqrt(2.0)
EXP2_SCALE = -0.5 / math.log(2.0)
EXP2_SHIFT = math.log2(2.0 / math.sqrt(2.0 * math.pi))
ROWS = 16
LANES = 128
NT = (((1,), (1,)), ((), ()))
VMEM_LIMIT = 60 << 20


def full_spec(array):
    return pl.BlockSpec(array.shape, lambda *_: (0,) * array.ndim)


def divisor(total, largest):
    return math.gcd(total, largest)


def split_low(values, pieces):
    found = []
    for _ in range(pieces):
        piece = values.astype(BF16).astype(F32)
        found.append(piece)
        values = values - piece
    return found


def as_rows(pieces, count):
    rows = lax.broadcasted_iota(jnp.int32, (count, pieces[0].shape[1]), 0)
    block = jnp.zeros(rows.shape, F32)
    for place, piece in enumerate(pieces):
        block = jnp.where(rows == place, piece, block)
    return block.astype(BF16)


def eye(size):
    rows = lax.broadcasted_iota(jnp.int32, (size, size), 0)
    return jnp.where(rows == lax.broadcasted_iota(jnp.int32, (size, size), 1), 1.0, 0.0).astype(BF16)


def transposed(block):
    return lax.dot_general(eye(block.shape[1]), block, NT, preferred_element_type=F32)


def gain_columns(gain_row):
    chans = gain_row.shape[1]
    total = None
    for piece in split_low(gain_row, 3):
        spread = jnp.broadcast_to(piece, (LANES, chans)).astype(BF16)
        part = lax.dot_general(eye(chans), spread, NT, preferred_element_type=F32)
        total = part if total is None else total + part
    return total


def widen(block, tile):
    return jnp.concatenate([block] * (tile // block.shape[1]), axis=1)


def other_sum(values, name):
    if lax.axis_size(name) == 2:
        return lax.ppermute(values, name, [(0, 1), (1, 0)])
    return lax.psum(values, name) - values


def unit_norm(values):
    centre = values - jnp.mean(values, axis=0, keepdims=True)
    inv_std = lax.rsqrt(jnp.mean(centre * centre, axis=0, keepdims=True) + 1e-05)
    return centre * inv_std, inv_std


def pack_kernel(k_ref, v_ref, q_ref, dout_ref, out_ref, norm_ref, send_ref, *, rows):
    targets, own_heads, _, keys = send_ref.shape
    head_dim = k_ref.shape[1]
    begin = 2 * head_dim
    for head in range(own_heads):
        dout = dout_ref[head]
        deltas = jnp.sum(dout.astype(F32) * out_ref[head].astype(F32), axis=0, keepdims=True)
        scalars = split_low(norm_ref[head : head + 1, :], 3) + split_low(deltas, 3)
        packed = jnp.concatenate([q_ref[head], dout, as_rows(scalars, ROWS)], axis=0)
        for target in range(targets):
            send_ref[target, head, :head_dim, :] = k_ref[head]
            send_ref[target, head, head_dim:begin, :] = v_ref[head]
            slab = target * rows // LANES * LANES
            pieces = [
                packed[place : place + ROWS, slab : slab + LANES] for place in range(0, packed.shape[0], ROWS)
            ]
            fill = keys - LANES * len(pieces)
            if fill:
                pieces.append(jnp.zeros((ROWS, fill), BF16))
            send_ref[target, head, begin:, :] = jnp.concatenate(pieces, axis=1)


def pack_call(k_heads, v_heads, q_heads, dout_heads, out_heads, log_norm, targets, rows):
    own_heads, head_dim, keys = k_heads.shape
    return pl.pallas_call(
        functools.partial(pack_kernel, rows=rows),
        out_shape=jax.ShapeDtypeStruct((targets, own_heads, 2 * head_dim + ROWS, keys), BF16),
        compiler_params=pltpu.CompilerParams(vmem_limit_bytes=VMEM_LIMIT),
        name="pack_heads",
    )(k_heads, v_heads, q_heads, dout_heads, out_heads, log_norm)


def forward_kernel(
    pair_ref, bucket_ref, gain_ref, w_in_ref, b_in_ref, w_out_ref, table_ref, slope_ref, bias_ref, w_pre, w_mix,
    w_table, gain, *, group, tile
):
    rows, chans, keys = pair_ref.shape
    heads, buckets = w_table.shape
    key_tiles = keys // tile
    first_row = pl.program_id(0) * rows

    @pl.when(pl.program_id(0) == 0)
    def _():
        stacked = jnp.concatenate([w_in_ref[...], as_rows(split_low(b_in_ref[...], 3), ROWS)], axis=0)
        w_pre[...] = transposed(stacked).astype(BF16)
        w_mix[...] = (lax.dot_general(eye(heads), w_out_ref[...], NT, preferred_element_type=F32) * 0.5).astype(BF16)
        w_table[...] = lax.dot_general(eye(heads), table_ref[...], NT, preferred_element_type=F32).astype(BF16)
        gain[...] = gain_columns(gain_ref[...])

    ones = jnp.where(lax.broadcasted_iota(jnp.int32, (ROWS, tile), 0) < 3, 1.0, 0.0).astype(BF16)

    def one_row(row, cols):
        unit_pairs, _ = unit_norm(pair_ref[row, :, cols].astype(F32))
        normed = (unit_pairs * widen(gain[...], tile)).astype(BF16)
        pre_act = jnp.dot(w_pre[...], jnp.concatenate([normed, ones], axis=0), preferred_element_type=F32)
        cdf2 = lax.erf(pre_act * RSQRT2) + 1.0
        hidden2 = (pre_act * cdf2).astype(BF16)
        density2 = jnp.exp2(pre_act * pre_act * EXP2_SCALE + EXP2_SHIFT)
        slope_ref[row, :, cols] = (cdf2 + pre_act * density2).astype(BF16)
        bucket_iota = lax.broadcasted_iota(jnp.int32, (buckets, tile), 0)
        onehot = jnp.where(bucket_ref[pl.ds(first_row + row, 1), cols] == bucket_iota, 1.0, 0.0).astype(BF16)
        mixed = jnp.dot(w_mix[...], hidden2, preferred_element_type=F32)
        return mixed + jnp.dot(w_table[...], onehot, preferred_element_type=F32)

    def step(index, carry):
        row_group = index // key_tiles
        cols = pl.ds(pl.multiple_of((index % key_tiles) * tile, tile), tile)
        outs = [one_row(row_group * group + member, cols) for member in range(group)]
        size = group * heads
        bias_ref[pl.ds(pl.multiple_of(row_group * size, size), size), cols] = jnp.concatenate(
            outs, axis=0
        ).astype(BF16)
        return carry

    lax.fori_loop(0, (rows // group) * key_tiles, step, 0)


def forward_call(pair_feats, bucket_ids, gain, w_in, b_in, w_out, table):
    rows, chans, keys = pair_feats.shape
    hid, heads = w_out.shape
    block = divisor(rows, 4)
    return pl.pallas_call(
        functools.partial(forward_kernel, group=block, tile=divisor(keys, 512)),
        grid=(rows // block,),
        in_specs=[
            pl.BlockSpec((block, chans, keys), lambda i: (i, 0, 0)),
            full_spec(bucket_ids),
            full_spec(gain),
            full_spec(w_in),
            full_spec(b_in),
            full_spec(w_out),
            full_spec(table),
        ],
        out_specs=[
            pl.BlockSpec((block, hid, keys), lambda i: (i, 0, 0)),
            pl.BlockSpec((block * heads, keys), lambda i: (i, 0)),
        ],
        out_shape=[
            jax.ShapeDtypeStruct((rows, hid, keys), BF16),
            jax.ShapeDtypeStruct((rows * heads, keys), BF16),
        ],
        scratch_shapes=[
            pltpu.VMEM((hid, chans + ROWS), BF16),
            pltpu.VMEM((heads, hid), BF16),
            pltpu.VMEM((heads, table.shape[0]), BF16),
            pltpu.VMEM((chans, LANES), F32),
        ],
        compiler_params=pltpu.CompilerParams(vmem_limit_bytes=VMEM_LIMIT),
        cost_estimate=pl.CostEstimate(
            flops=2 * rows * keys * hid * 256,
            bytes_accessed=2 * rows * keys * (hid + chans),
            transcendentals=2 * rows * keys * hid,
        ),
        name="pair_forward",
    )(pair_feats, bucket_ids, gain, w_in, b_in, w_out, table)


def attention_kernel(
    bias_ref, kv_ref, aux_ref, mask_ref, ds_ref, part_ref, q_rows, d_rows, q_cols, d_cols, norm_ref, delta_ref,
    dq_acc, *, head_dim, rows
):
    heads = kv_ref.shape[0]
    tile = bias_ref.shape[1]
    width = heads * head_dim
    flat = rows * heads
    scale = 1.0 / math.sqrt(head_dim)
    step = pl.program_id(0)
    cols = pl.ds(pl.multiple_of(step * tile, tile), tile)
    offset = lax.rem(lax.axis_index("heads") * rows, LANES)
    groups = head_dim // ROWS

    def spread_matrix():
        lane = lax.broadcasted_iota(jnp.int32, (flat, LANES), 1)
        return lane == lax.broadcasted_iota(jnp.int32, (flat, LANES), 0) // heads + offset

    def own_columns():
        return (
            lax.broadcasted_iota(jnp.int32, (width, flat), 1) % heads
            == lax.broadcasted_iota(jnp.int32, (width, flat), 0) // head_dim
        )

    @pl.when(step == 0)
    def _():
        spread_low = jnp.where(spread_matrix(), 1.0, 0.0).astype(BF16)
        own_rows = (
            lax.broadcasted_iota(jnp.int32, (flat, width), 0) % heads
            == lax.broadcasted_iota(jnp.int32, (flat, width), 1) // head_dim
        )
        own_cols = own_columns()
        for begin, by_rows, by_cols in ((0, q_rows, q_cols), (groups, d_rows, d_cols)):
            block = jnp.concatenate(
                [aux_ref[:, :, (begin + part) * LANES : (begin + part + 1) * LANES] for part in range(groups)], axis=1
            ).reshape(width, LANES)
            spread = lax.dot_general(spread_low, block, NT, preferred_element_type=F32)
            by_rows[...] = jnp.where(own_rows, spread, 0.0).astype(BF16)
            spread = lax.dot_general(block, spread_low, NT, preferred_element_type=F32)
            by_cols[...] = jnp.where(own_cols, spread, 0.0).astype(BF16)
        tail = aux_ref[:, :, 2 * groups * LANES : (2 * groups + 1) * LANES].astype(F32)
        lane = lax.broadcasted_iota(jnp.int32, (rows, heads, LANES), 2)
        own_lane = lane == lax.broadcasted_iota(jnp.int32, (rows, heads, LANES), 0) + offset
        for begin, target in ((0, norm_ref), (3, delta_ref)):
            pieces = tail[:, begin, :] + tail[:, begin + 1, :] + tail[:, begin + 2, :]
            column = jnp.sum(jnp.where(own_lane, pieces[None], 0.0), axis=2, keepdims=True)
            target[...] = jnp.broadcast_to(column.reshape(flat, 1), target.shape)
        dq_acc[...] = jnp.zeros_like(dq_acc)

    norm = widen(norm_ref[...], tile)
    delta = widen(delta_ref[...], tile)
    keys = kv_ref[:, :head_dim, :].reshape(width, tile)
    values = kv_ref[:, head_dim:, :].reshape(width, tile)
    scores = jnp.dot(q_rows[...], keys, preferred_element_type=F32) * scale + bias_ref[...].astype(F32)
    probs = jnp.where(mask_ref[...] == 1, jnp.exp(scores - norm), 0.0)
    dprobs = jnp.dot(d_rows[...], values, preferred_element_type=F32)
    dscores = (probs * (dprobs - delta)).astype(BF16)
    ds_ref[...] = dscores
    dk_part = jnp.dot(q_cols[...], dscores, preferred_element_type=F32)
    dv_part = jnp.dot(d_cols[...], probs.astype(BF16), preferred_element_type=F32)
    part_ref[:, :head_dim, cols] = dk_part.reshape(heads, head_dim, tile).astype(BF16)
    part_ref[:, head_dim : 2 * head_dim, cols] = dv_part.reshape(heads, head_dim, tile).astype(BF16)
    dq_acc[...] += lax.dot_general(keys, dscores, NT, preferred_element_type=F32)

    @pl.when(step == pl.num_programs(0) - 1)
    def _():
        spread_low = jnp.where(spread_matrix(), 1.0, 0.0).astype(BF16)
        total = None
        for piece in split_low(jnp.where(own_columns(), dq_acc[...], 0.0), 3):
            part = jnp.dot(piece.astype(BF16), spread_low, preferred_element_type=F32)
            total = part if total is None else total + part
        pieces = []
        for piece in split_low(total, 2):
            block = piece.astype(BF16).reshape(heads, head_dim, LANES)
            pieces += [block[:, place : place + ROWS, :] for place in range(0, head_dim, ROWS)]
        fill = part_ref.shape[2] - LANES * len(pieces)
        if fill:
            pieces.append(jnp.zeros((heads, ROWS, fill), BF16))
        part_ref[:, 2 * head_dim :, :] = jnp.concatenate(pieces, axis=2)


def attention_call(bias, received, key_mask, head_dim, rows):
    flat, keys = bias.shape
    heads, depth, _ = received.shape
    width = heads * head_dim
    tile = divisor(keys, 256)
    return pl.pallas_call(
        functools.partial(attention_kernel, head_dim=head_dim, rows=rows),
        grid=(keys // tile,),
        in_specs=[
            pl.BlockSpec((flat, tile), lambda i: (0, i)),
            pl.BlockSpec((heads, 2 * head_dim, tile), lambda i: (0, 0, i)),
            pl.BlockSpec((heads, ROWS, keys), lambda i: (0, 2 * head_dim // ROWS, 0)),
            pl.BlockSpec((1, tile), lambda i: (0, i)),
        ],
        out_specs=[
            pl.BlockSpec((flat, tile), lambda i: (0, i)),
            pl.BlockSpec((heads, depth, keys), lambda i: (0, 0, 0)),
        ],
        out_shape=[
            jax.ShapeDtypeStruct((flat, keys), BF16),
            jax.ShapeDtypeStruct((heads, depth, keys), BF16),
        ],
        scratch_shapes=[
            pltpu.VMEM((flat, width), BF16),
            pltpu.VMEM((flat, width), BF16),
            pltpu.VMEM((width, flat), BF16),
            pltpu.VMEM((width, flat), BF16),
            pltpu.VMEM((flat, LANES), F32),
            pltpu.VMEM((flat, LANES), F32),
            pltpu.VMEM((width, flat), F32),
        ],
        compiler_params=pltpu.CompilerParams(vmem_limit_bytes=VMEM_LIMIT),
        cost_estimate=pl.CostEstimate(
            flops=10 * flat * keys * width, bytes_accessed=8 * flat * keys, transcendentals=flat * keys
        ),
        name="pair_attention",
    )(bias, received, received, key_mask.reshape(1, keys))


def backward_kernel(
    pair_ref, ds_ref, slope_ref, gain_ref, w_in_ref, w_out_ref, *rest, group, tile
):
    out_ref, w_back, gain = rest[-3:]
    rows, chans, keys = pair_ref.shape
    heads = w_back.shape[1]
    key_tiles = keys // tile

    @pl.when(pl.program_id(0) == 0)
    def _():
        w_back[...] = (w_out_ref[...].astype(F32) * 0.5).astype(BF16)
        gain[...] = gain_columns(gain_ref[...])

    def step(index, carry):
        row_group = index // key_tiles
        cols = pl.ds(pl.multiple_of((index % key_tiles) * tile, tile), tile)
        size = group * heads
        dscores = ds_ref[pl.ds(pl.multiple_of(row_group * size, size), size), cols]
        for member in range(group):
            row = row_group * group + member
            unit_pairs, inv_std = unit_norm(pair_ref[row, :, cols].astype(F32))
            dhidden = jnp.dot(
                w_back[...], dscores[member * heads : (member + 1) * heads], preferred_element_type=F32
            )
            dpre = dhidden.astype(BF16) * slope_ref[row, :, cols]
            dunit = jnp.dot(w_in_ref[...], dpre, preferred_element_type=F32) * widen(gain[...], tile)
            first_mean = jnp.mean(dunit, axis=0, keepdims=True)
            second_mean = jnp.mean(dunit * unit_pairs, axis=0, keepdims=True)
            grad = inv_std * (dunit - first_mean - unit_pairs * second_mean)
            out_ref[row, :, cols] = grad.astype(BF16)
        return carry

    lax.fori_loop(0, (rows // group) * key_tiles, step, 0)


def backward_call(pair_feats, dscores, slope, gain, w_in, w_out, begin, count, previous):
    rows, chans, keys = pair_feats.shape
    hid, heads = w_out.shape
    block = divisor(math.gcd(begin, count), 4)
    first = begin // block
    operands = [pair_feats, dscores, slope, gain, w_in, w_out]
    in_specs = [
        pl.BlockSpec((block, chans, keys), lambda i: (i + first, 0, 0)),
        pl.BlockSpec((block * heads, keys), lambda i: (i + first, 0)),
        pl.BlockSpec((block, hid, keys), lambda i: (i + first, 0, 0)),
        full_spec(gain),
        full_spec(w_in),
        full_spec(w_out),
    ]
    aliases = {}
    if previous is not None:
        aliases = {len(operands): 0}
        operands.append(previous)
        in_specs.append(pl.BlockSpec(memory_space=pl.ANY))
    return pl.pallas_call(
        functools.partial(backward_kernel, group=block, tile=divisor(keys, 512)),
        grid=(count // block,),
        in_specs=in_specs,
        out_specs=pl.BlockSpec((block, chans, keys), lambda i: (i + first, 0, 0)),
        out_shape=jax.ShapeDtypeStruct((rows, chans, keys), BF16),
        scratch_shapes=[pltpu.VMEM((hid, heads), BF16), pltpu.VMEM((chans, LANES), F32)],
        input_output_aliases=aliases,
        compiler_params=pltpu.CompilerParams(vmem_limit_bytes=VMEM_LIMIT),
        cost_estimate=pl.CostEstimate(
            flops=2 * count * keys * hid * 256,
            bytes_accessed=2 * count * keys * (hid + 2 * chans),
            transcendentals=0,
        ),
        name="pair_backward",
    )(*operands)


def sum_kernel(part_ref, dkv_ref, dq_ref, *, head_dim, rows):
    sources, own_heads, _, keys = part_ref.shape
    for head in range(own_heads):
        total = part_ref[0, head, : 2 * head_dim, :].astype(F32)
        for source in range(1, sources):
            total = total + part_ref[source, head, : 2 * head_dim, :].astype(F32)
        dkv_ref[head] = total
        dq_ref[head] = jnp.zeros(dq_ref.shape[1:], F32)
        for source in range(sources):
            slab = source * rows // LANES * LANES
            groups = head_dim // ROWS
            for part in range(2 * groups):
                piece = part_ref[source, head, 2 * head_dim :, part * LANES : (part + 1) * LANES].astype(F32)
                place = part % groups * ROWS
                dq_ref[head, place : place + ROWS, slab : slab + LANES] += piece


def sum_call(parts, head_dim, rows, queries):
    _, own_heads, _, keys = parts.shape
    return pl.pallas_call(
        functools.partial(sum_kernel, head_dim=head_dim, rows=rows),
        out_shape=[
            jax.ShapeDtypeStruct((own_heads, 2 * head_dim, keys), F32),
            jax.ShapeDtypeStruct((own_heads, head_dim, queries), F32),
        ],
        compiler_params=pltpu.CompilerParams(vmem_limit_bytes=VMEM_LIMIT),
        name="sum_sources",
    )(parts)


def finish_kernel(dkv_ref, dkv_other, dq_ref, dq_other, grad_q, grad_k, grad_v, *, head_dim):
    scale = 1.0 / math.sqrt(head_dim)
    total = dkv_ref[...] + dkv_other[...]
    grad_q[...] = ((dq_ref[...] + dq_other[...]) * scale).astype(BF16)
    grad_k[...] = (total[:, :head_dim, :] * scale).astype(BF16)
    grad_v[...] = total[:, head_dim:, :].astype(BF16)


def finish_call(dkv, dkv_other, dq, dq_other):
    own_heads, head_dim, queries = dq.shape
    keys = dkv.shape[2]
    return pl.pallas_call(
        functools.partial(finish_kernel, head_dim=head_dim),
        out_shape=[
            jax.ShapeDtypeStruct((own_heads, head_dim, queries), BF16),
            jax.ShapeDtypeStruct((own_heads, head_dim, keys), BF16),
            jax.ShapeDtypeStruct((own_heads, head_dim, keys), BF16),
        ],
        compiler_params=pltpu.CompilerParams(vmem_limit_bytes=VMEM_LIMIT),
        name="finish",
    )(dkv, dkv_other, dq, dq_other)


def per_device(
    pair_feats,
    bucket_ids,
    ln_gain,
    w_in,
    b_in,
    w_out,
    bucket_table,
    key_mask,
    q_heads,
    k_heads,
    v_heads,
    out_heads,
    dout_heads,
    log_norm,
):
    axis_size = lax.axis_size("heads")
    own_heads, head_dim, queries = q_heads.shape
    rows = pair_feats.shape[0]
    gain = ln_gain.reshape(1, -1)

    packed = pack_call(k_heads, v_heads, q_heads, dout_heads, out_heads, log_norm, axis_size, rows)
    received = lax.all_to_all(packed, "heads", split_axis=0, concat_axis=0, tiled=True)
    slope, bias_vals = forward_call(
        pair_feats, bucket_ids, gain, w_in, b_in.reshape(1, -1), w_out, bucket_table
    )
    received = received.reshape((axis_size * own_heads,) + received.shape[2:])
    dscores, parts = attention_call(bias_vals, received, key_mask, head_dim, rows)
    parts = lax.all_to_all(
        parts.reshape((axis_size, own_heads) + parts.shape[1:]), "heads", split_axis=0, concat_axis=0, tiled=True
    )
    last = rows // 4
    weights = (gain, w_in, w_out)
    grad_pairs = backward_call(pair_feats, dscores, slope, *weights, 0, rows - last, None)
    parts, grad_pairs = lax.optimization_barrier((parts, grad_pairs))
    dkv_sum, dq_sum = sum_call(parts, head_dim, rows, queries)
    grad_pairs, dkv_sum, dq_sum = lax.optimization_barrier((grad_pairs, dkv_sum, dq_sum))
    dkv_other = other_sum(dkv_sum, "query")
    dq_other = other_sum(dq_sum, "key")
    grad_pairs = backward_call(pair_feats, dscores, slope, *weights, rows - last, last, grad_pairs)
    grad_q, grad_k, grad_v = finish_call(dkv_sum, dkv_other, dq_sum, dq_other)
    return (grad_pairs, grad_q, grad_k, grad_v)


def solution(mesh):
    def traced(*args):
        with jax.sharding.use_abstract_mesh(mesh.abstract_mesh):
            return jax.shard_map(
                per_device,
                mesh=mesh,
                in_specs=(
                    P(("query", "heads"), None, "key"),
                    P(("query", "heads"), "key"),
                    P(),
                    P(),
                    P(),
                    P(),
                    P(),
                    P("key"),
                    P("heads", None, "query"),
                    P("heads", None, "key"),
                    P("heads", None, "key"),
                    P("heads", None, "query"),
                    P("heads", None, "query"),
                    P("heads", "query"),
                ),
                out_specs=(
                    P(("query", "heads"), None, "key"),
                    P("heads", None, "query"),
                    P("heads", None, "key"),
                    P("heads", None, "key"),
                ),
                check_vma=False,
            )(*args)

    return traced
```

```python
import functools
import math

import jax
import jax.numpy as jnp
from jax import lax
from jax.experimental import pallas as pl
from jax.experimental.pallas import tpu as pltpu
from jax.sharding import PartitionSpec as P

F32 = jnp.float32
BF16 = jnp.bfloat16
RSQRT2 = 1.0 / math.sqrt(2.0)
EXP2_SCALE = -0.5 / math.log(2.0)
EXP2_SHIFT = math.log2(2.0 / math.sqrt(2.0 * math.pi))
ROWS = 16
LANES = 128
NT = (((1,), (1,)), ((), ()))
FULL_LIMIT = 60 << 20
BIG_LIMIT = 32 << 20
SMALL_LIMIT = 16 << 20


def low(value):
    return jnp.asarray(value, BF16)


def full_spec(array):
    return pl.BlockSpec(array.shape, lambda *_: (0,) * array.ndim)


def divisor(total, largest):
    return math.gcd(total, largest)


def split_low(values, pieces):
    found = []
    for _ in range(pieces):
        piece = values.astype(BF16).astype(F32)
        found.append(piece)
        values = values - piece
    return found


def as_rows(pieces, count):
    rows = lax.broadcasted_iota(jnp.int32, (count, pieces[0].shape[1]), 0)
    block = jnp.zeros(rows.shape, F32)
    for place, piece in enumerate(pieces):
        block = jnp.where(rows == place, piece, block)
    return block.astype(BF16)


def eye(size):
    rows = lax.broadcasted_iota(jnp.int32, (size, size), 0)
    return jnp.where(rows == lax.broadcasted_iota(jnp.int32, (size, size), 1), 1.0, 0.0).astype(BF16)


def transposed(block):
    return lax.dot_general(eye(block.shape[1]), block, NT, preferred_element_type=F32)


def gain_columns(gain_row):
    chans = gain_row.shape[1]
    total = None
    for piece in split_low(gain_row, 3):
        spread = jnp.broadcast_to(piece, (LANES, chans)).astype(BF16)
        part = lax.dot_general(eye(chans), spread, NT, preferred_element_type=F32)
        total = part if total is None else total + part
    return total


def widen(block, tile):
    return jnp.concatenate([block] * (tile // block.shape[1]), axis=1)


def other_sum(values, name):
    if lax.axis_size(name) == 2:
        return lax.ppermute(values, name, [(0, 1), (1, 0)])
    return lax.psum(values, name) - values


def pack_kernel(k_ref, v_ref, q_ref, dout_ref, out_ref, norm_ref, send_ref, *, rows):
    targets, own_heads, depth, lanes = send_ref.shape
    head_dim = k_ref.shape[1]
    keys = lanes - LANES
    half = LANES // 2
    lane = lax.broadcasted_iota(jnp.int32, (depth, LANES), 1)
    for head in range(own_heads):
        dout = dout_ref[head]
        deltas = jnp.sum(dout.astype(F32) * out_ref[head].astype(F32), axis=0, keepdims=True)
        scalars = as_rows(split_low(norm_ref[head : head + 1, :], 3) + split_low(deltas, 3), depth).astype(F32)
        heads_part = jnp.concatenate([q_ref[head], dout], axis=0).astype(F32)
        for target in range(targets):
            send_ref[target, head, :head_dim, :keys] = k_ref[head]
            send_ref[target, head, head_dim:, :keys] = v_ref[head]
            slab = target * rows // LANES * LANES
            window = (lane >= target * rows - slab) & (lane < target * rows - slab + rows)
            turned = [scalars[:, slab + half : slab + LANES], scalars[:, slab : slab + half]]
            extra = jnp.where(window, heads_part[:, slab : slab + LANES], jnp.concatenate(turned, axis=1))
            send_ref[target, head, :, keys:] = extra.astype(BF16)


def pack_call(k_heads, v_heads, q_heads, dout_heads, out_heads, log_norm, targets, rows):
    own_heads, head_dim, keys = k_heads.shape
    return pl.pallas_call(
        functools.partial(pack_kernel, rows=rows),
        out_shape=jax.ShapeDtypeStruct((targets, own_heads, 2 * head_dim, keys + LANES), BF16),
        compiler_params=pltpu.CompilerParams(vmem_limit_bytes=FULL_LIMIT),
        name="pack_heads",
    )(k_heads, v_heads, q_heads, dout_heads, out_heads, log_norm)


def unit_norm(values):
    centre = values - jnp.mean(values, axis=0, keepdims=True)
    inv_std = lax.rsqrt(jnp.mean(centre * centre, axis=0, keepdims=True) + 1e-05)
    return centre * inv_std, inv_std


def forward_kernel(
    pair_ref, bucket_ref, gain_ref, w_in_ref, b_in_ref, w_out_ref, table_ref, pre_ref, bias_ref, w_pre, w_mix, table,
    gain, *, group, merge
):
    rows, chans, keys = pair_ref.shape
    heads, buckets = table_ref.shape
    width = merge * keys
    first_row = pl.program_id(0) * rows

    @pl.when(pl.program_id(0) == 0)
    def _():
        stacked = jnp.concatenate([w_in_ref[...], as_rows(split_low(b_in_ref[...], 3), ROWS)], axis=0)
        w_pre[...] = transposed(stacked).astype(BF16)
        w_mix[...] = (w_out_ref[...].astype(F32) * 0.5).astype(BF16)
        place = jnp.where(
            lax.broadcasted_iota(jnp.int32, (buckets, LANES), 0) == lax.broadcasted_iota(jnp.int32, (buckets, LANES), 1),
            1.0,
            0.0,
        ).astype(BF16)
        table[...] = jnp.dot(table_ref[...], place, preferred_element_type=F32)
        gain[...] = gain_columns(gain_ref[...])

    def some_rows(row):
        pairs = jnp.concatenate([pair_ref[row + member] for member in range(merge)], axis=1)
        unit_pairs, _ = unit_norm(pairs.astype(F32))
        normed = (unit_pairs * widen(gain[...], width)).astype(BF16)
        ones = jnp.where(lax.broadcasted_iota(jnp.int32, (ROWS, width), 0) < 3, 1.0, 0.0).astype(BF16)
        pre_act = jnp.dot(w_pre[...], jnp.concatenate([normed, ones], axis=0), preferred_element_type=F32)
        hidden = (pre_act * (lax.erf(pre_act * RSQRT2) + 1.0)).astype(BF16)
        pre_low = pre_act.astype(BF16)
        outs = []
        mixed = jnp.dot(w_mix[...], hidden, preferred_element_type=F32)
        for member in range(merge):
            pieces = []
            id_row = bucket_ref[pl.ds(first_row + row + member, 1), :]
            for part in range(keys // LANES):
                begin = member * keys + part * LANES
                pre_ref[row + member, part] = pre_low[:, begin : begin + LANES]
                ids = id_row[:, part * LANES : (part + 1) * LANES]
                lookup = jnp.take_along_axis(table[...], jnp.broadcast_to(ids, (heads, LANES)), axis=1)
                pieces.append(mixed[:, begin : begin + LANES] + lookup)
            outs.append(jnp.concatenate(pieces, axis=1))
        return outs

    def step(index, carry):
        outs = []
        for member in range(0, group, merge):
            outs += some_rows(index * group + member)
        size = group * heads
        bias_ref[pl.ds(pl.multiple_of(index * size, size), size), :] = jnp.concatenate(outs, axis=0).astype(BF16)
        return carry

    lax.fori_loop(0, rows // group, step, 0)


def forward_call(pair_feats, bucket_ids, gain, w_in, b_in, w_out, table):
    rows, chans, keys = pair_feats.shape
    heads, hid = w_out.shape
    block = divisor(rows, 8)
    parts = keys // LANES
    return pl.pallas_call(
        functools.partial(forward_kernel, group=block, merge=divisor(block, 2)),
        grid=(rows // block,),
        in_specs=[
            pl.BlockSpec((block, chans, keys), lambda i: (i, 0, 0)),
            full_spec(bucket_ids),
            full_spec(gain),
            full_spec(w_in),
            full_spec(b_in),
            full_spec(w_out),
            full_spec(table),
        ],
        out_specs=[
            pl.BlockSpec((block, parts, hid, LANES), lambda i: (i, 0, 0, 0)),
            pl.BlockSpec((block * heads, keys), lambda i: (i, 0)),
        ],
        out_shape=[
            jax.ShapeDtypeStruct((rows, parts, hid, LANES), BF16),
            jax.ShapeDtypeStruct((rows * heads, keys), BF16),
        ],
        scratch_shapes=[
            pltpu.VMEM((hid, chans + ROWS), BF16),
            pltpu.VMEM((heads, hid), BF16),
            pltpu.VMEM((heads, LANES), F32),
            pltpu.VMEM((chans, LANES), F32),
        ],
        compiler_params=pltpu.CompilerParams(vmem_limit_bytes=FULL_LIMIT),
        cost_estimate=pl.CostEstimate(
            flops=2 * rows * keys * hid * 256,
            bytes_accessed=2 * rows * keys * (hid + chans),
            transcendentals=2 * rows * keys * hid,
        ),
        name="pair_forward",
    )(pair_feats, bucket_ids, gain, w_in, b_in, w_out, table)


def attention_kernel(
    bias_ref, kv_ref, aux_ref, mask_ref, ds_ref, part_ref, q_rows, d_rows, q_cols, d_cols, norm_ref, delta_ref,
    dq_acc, *, head_dim, rows
):
    heads = kv_ref.shape[0]
    tile = bias_ref.shape[1]
    width = heads * head_dim
    flat = rows * heads
    scale = 1.0 / math.sqrt(head_dim)
    step = pl.program_id(0)
    cols = pl.ds(pl.multiple_of(step * tile, tile), tile)
    offset = lax.rem(lax.axis_index("heads") * rows, LANES)
    scalar_offset = lax.rem(offset + LANES // 2, LANES)

    def spread_matrix():
        lane = lax.broadcasted_iota(jnp.int32, (flat, LANES), 1)
        return lane == lax.broadcasted_iota(jnp.int32, (flat, LANES), 0) // heads + offset

    def own_columns():
        return (
            lax.broadcasted_iota(jnp.int32, (width, flat), 1) % heads
            == lax.broadcasted_iota(jnp.int32, (width, flat), 0) // head_dim
        )

    @pl.when(step == 0)
    def _():
        spread_low = jnp.where(spread_matrix(), 1.0, 0.0).astype(BF16)
        own_rows = (
            lax.broadcasted_iota(jnp.int32, (flat, width), 0) % heads
            == lax.broadcasted_iota(jnp.int32, (flat, width), 1) // head_dim
        )
        own_cols = own_columns()
        for begin, by_rows, by_cols in ((0, q_rows, q_cols), (head_dim, d_rows, d_cols)):
            block = aux_ref[:, begin : begin + head_dim, :].reshape(width, LANES)
            spread = lax.dot_general(spread_low, block, NT, preferred_element_type=F32)
            by_rows[...] = jnp.where(own_rows, spread, 0.0).astype(BF16)
            spread = lax.dot_general(block, spread_low, NT, preferred_element_type=F32)
            by_cols[...] = jnp.where(own_cols, spread, 0.0).astype(BF16)
        tail = aux_ref[:, :ROWS, :].astype(F32)
        lane = lax.broadcasted_iota(jnp.int32, (rows, heads, LANES), 2)
        own_lane = lane == lax.broadcasted_iota(jnp.int32, (rows, heads, LANES), 0) + scalar_offset
        for begin, target in ((0, norm_ref), (3, delta_ref)):
            pieces = tail[:, begin, :] + tail[:, begin + 1, :] + tail[:, begin + 2, :]
            column = jnp.sum(jnp.where(own_lane, pieces[None], 0.0), axis=2, keepdims=True)
            target[...] = jnp.broadcast_to(column.reshape(flat, 1), target.shape)
        dq_acc[...] = jnp.zeros_like(dq_acc)

    norm = widen(norm_ref[...], tile)
    delta = widen(delta_ref[...], tile)
    keys = kv_ref[:, :head_dim, :].reshape(width, tile)
    values = kv_ref[:, head_dim:, :].reshape(width, tile)
    scores = jnp.dot(q_rows[...], keys, preferred_element_type=F32) * scale + bias_ref[...].astype(F32)
    probs = jnp.where(mask_ref[...] == 1, jnp.exp(scores - norm), 0.0)
    dprobs = jnp.dot(d_rows[...], values, preferred_element_type=F32)
    dscores = (probs * (dprobs - delta)).astype(BF16)
    ds_ref[...] = dscores
    dk_part = jnp.dot(q_cols[...], dscores, preferred_element_type=F32)
    dv_part = jnp.dot(d_cols[...], probs.astype(BF16), preferred_element_type=F32)
    part_ref[:, :head_dim, cols] = dk_part.reshape(heads, head_dim, tile).astype(BF16)
    part_ref[:, head_dim : 2 * head_dim, cols] = dv_part.reshape(heads, head_dim, tile).astype(BF16)
    dq_acc[...] += lax.dot_general(keys, dscores, NT, preferred_element_type=F32)

    @pl.when(step == pl.num_programs(0) - 1)
    def _():
        spread_low = jnp.where(spread_matrix(), 1.0, 0.0).astype(BF16)
        total = None
        for piece in split_low(jnp.where(own_columns(), dq_acc[...], 0.0), 3):
            part = jnp.dot(piece.astype(BF16), spread_low, preferred_element_type=F32)
            total = part if total is None else total + part
        high, rest = split_low(total, 2)
        keys_end = part_ref.shape[2] - LANES
        part_ref[:, :head_dim, keys_end:] = high.astype(BF16).reshape(heads, head_dim, LANES)
        part_ref[:, head_dim:, keys_end:] = rest.astype(BF16).reshape(heads, head_dim, LANES)


def attention_call(bias, received, key_mask, head_dim, rows):
    flat, keys = bias.shape
    heads, depth, _ = received.shape
    width = heads * head_dim
    tile = divisor(keys, 256)
    return pl.pallas_call(
        functools.partial(attention_kernel, head_dim=head_dim, rows=rows),
        grid=(keys // tile,),
        in_specs=[
            pl.BlockSpec((flat, tile), lambda i: (0, i)),
            pl.BlockSpec((heads, 2 * head_dim, tile), lambda i: (0, 0, i)),
            pl.BlockSpec((heads, depth, LANES), lambda i: (0, 0, keys // LANES)),
            pl.BlockSpec((1, tile), lambda i: (0, i)),
        ],
        out_specs=[
            pl.BlockSpec((flat, tile), lambda i: (0, i)),
            pl.BlockSpec((heads, depth, keys + LANES), lambda i: (0, 0, 0)),
        ],
        out_shape=[
            jax.ShapeDtypeStruct((flat, keys), BF16),
            jax.ShapeDtypeStruct((heads, depth, keys + LANES), BF16),
        ],
        scratch_shapes=[
            pltpu.VMEM((flat, width), BF16),
            pltpu.VMEM((flat, width), BF16),
            pltpu.VMEM((width, flat), BF16),
            pltpu.VMEM((width, flat), BF16),
            pltpu.VMEM((flat, LANES), F32),
            pltpu.VMEM((flat, LANES), F32),
            pltpu.VMEM((width, flat), F32),
        ],
        compiler_params=pltpu.CompilerParams(vmem_limit_bytes=BIG_LIMIT),
        cost_estimate=pl.CostEstimate(
            flops=10 * flat * keys * width, bytes_accessed=8 * flat * keys, transcendentals=flat * keys
        ),
        name="pair_attention",
    )(bias, received, received, key_mask.reshape(1, keys))


def backward_kernel(pair_ref, ds_ref, pre_ref, gain_ref, w_in_ref, w_out_ref, *rest, group):
    out_ref, w_back, gain = rest[-3:]
    rows, chans, keys = pair_ref.shape
    heads = w_out_ref.shape[0]
    parts = keys // LANES

    @pl.when(pl.program_id(0) == 0)
    def _():
        w_back[...] = (transposed(w_out_ref[...]) * 0.5).astype(BF16)
        gain[...] = gain_columns(gain_ref[...])

    def step(index, carry):
        size = group * heads
        dscores = ds_ref[pl.ds(pl.multiple_of(index * size, size), size), :]
        for member in range(group):
            row = index * group + member
            unit_pairs, inv_std = unit_norm(pair_ref[row].astype(F32))
            pre_act = jnp.concatenate([pre_ref[row, part] for part in range(parts)], axis=1)
            dhidden = jnp.dot(
                w_back[...], dscores[member * heads : (member + 1) * heads], preferred_element_type=F32
            )
            cdf2 = lax.erf(pre_act * low(RSQRT2)) + low(1.0)
            density2 = jnp.exp2(pre_act * pre_act * low(EXP2_SCALE) + low(EXP2_SHIFT))
            dpre = dhidden.astype(BF16) * (cdf2 + pre_act * density2)
            dunit = jnp.dot(w_in_ref[...], dpre, preferred_element_type=F32) * widen(gain[...], keys)
            first_mean = jnp.mean(dunit, axis=0, keepdims=True)
            second_mean = jnp.mean(dunit * unit_pairs, axis=0, keepdims=True)
            out_ref[row] = (inv_std * (dunit - first_mean - unit_pairs * second_mean)).astype(BF16)
        return carry

    lax.fori_loop(0, rows // group, step, 0)


def backward_call(pair_feats, dscores, pre_act, gain, w_in, w_out, begin, count, previous):
    rows, chans, keys = pair_feats.shape
    parts = keys // LANES
    heads, hid = w_out.shape
    block = divisor(math.gcd(begin, count), 8)
    first = begin // block
    operands = [pair_feats, dscores, pre_act, gain, w_in, w_out]
    in_specs = [
        pl.BlockSpec((block, chans, keys), lambda i: (i + first, 0, 0)),
        pl.BlockSpec((block * heads, keys), lambda i: (i + first, 0)),
        pl.BlockSpec((block, parts, hid, LANES), lambda i: (i + first, 0, 0, 0)),
        full_spec(gain),
        full_spec(w_in),
        full_spec(w_out),
    ]
    aliases = {}
    if previous is not None:
        aliases = {len(operands): 0}
        operands.append(previous)
        in_specs.append(pl.BlockSpec(memory_space=pl.ANY))
    return pl.pallas_call(
        functools.partial(backward_kernel, group=block),
        grid=(count // block,),
        in_specs=in_specs,
        out_specs=pl.BlockSpec((block, chans, keys), lambda i: (i + first, 0, 0)),
        out_shape=jax.ShapeDtypeStruct((rows, chans, keys), BF16),
        scratch_shapes=[pltpu.VMEM((hid, heads), BF16), pltpu.VMEM((chans, LANES), F32)],
        input_output_aliases=aliases,
        compiler_params=pltpu.CompilerParams(vmem_limit_bytes=FULL_LIMIT),
        cost_estimate=pl.CostEstimate(
            flops=2 * count * keys * hid * 256,
            bytes_accessed=2 * count * keys * (hid + 2 * chans),
            transcendentals=0,
        ),
        name="pair_backward",
    )(*operands)


def sum_kernel(part_ref, dkv_ref, dq_ref, *, head_dim, rows):
    sources, own_heads, _, lanes = part_ref.shape
    keys = lanes - LANES
    for head in range(own_heads):
        total = part_ref[0, head, :, :keys].astype(F32)
        for source in range(1, sources):
            total = total + part_ref[source, head, :, :keys].astype(F32)
        dkv_ref[head] = total
        dq_ref[head] = jnp.zeros(dq_ref.shape[1:], F32)
        for source in range(sources):
            slab = source * rows // LANES * LANES
            piece = part_ref[source, head, :, keys:].astype(F32)
            dq_ref[head, :, slab : slab + LANES] += piece[:head_dim] + piece[head_dim:]


def sum_call(parts, head_dim, rows, queries):
    _, own_heads, _, lanes = parts.shape
    return pl.pallas_call(
        functools.partial(sum_kernel, head_dim=head_dim, rows=rows),
        out_shape=[
            jax.ShapeDtypeStruct((own_heads, 2 * head_dim, lanes - LANES), F32),
            jax.ShapeDtypeStruct((own_heads, head_dim, queries), F32),
        ],
        compiler_params=pltpu.CompilerParams(vmem_limit_bytes=SMALL_LIMIT),
        name="sum_sources",
    )(parts)


def finish_kernel(dkv_ref, dkv_other, dq_ref, dq_other, grad_q, grad_k, grad_v, *, head_dim):
    scale = 1.0 / math.sqrt(head_dim)
    total = dkv_ref[...] + dkv_other[...]
    grad_q[...] = ((dq_ref[...] + dq_other[...]) * scale).astype(BF16)
    grad_k[...] = (total[:, :head_dim, :] * scale).astype(BF16)
    grad_v[...] = total[:, head_dim:, :].astype(BF16)


def finish_call(dkv, dkv_other, dq, dq_other):
    own_heads, head_dim, queries = dq.shape
    keys = dkv.shape[2]
    return pl.pallas_call(
        functools.partial(finish_kernel, head_dim=head_dim),
        out_shape=[
            jax.ShapeDtypeStruct((own_heads, head_dim, queries), BF16),
            jax.ShapeDtypeStruct((own_heads, head_dim, keys), BF16),
            jax.ShapeDtypeStruct((own_heads, head_dim, keys), BF16),
        ],
        compiler_params=pltpu.CompilerParams(vmem_limit_bytes=SMALL_LIMIT),
        name="finish",
    )(dkv, dkv_other, dq, dq_other)


def per_device(
    pair_feats,
    bucket_ids,
    ln_gain,
    w_in,
    b_in,
    w_out,
    bucket_table,
    key_mask,
    q_heads,
    k_heads,
    v_heads,
    out_heads,
    dout_heads,
    log_norm,
):
    axis_size = lax.axis_size("heads")
    own_heads, head_dim, queries = q_heads.shape
    rows = pair_feats.shape[0]
    gain = ln_gain.reshape(1, -1)

    packed = pack_call(k_heads, v_heads, q_heads, dout_heads, out_heads, log_norm, axis_size, rows)
    received = lax.all_to_all(packed, "heads", split_axis=0, concat_axis=0, tiled=True)
    pre_act, bias_vals = forward_call(
        pair_feats, bucket_ids, gain, w_in, b_in.reshape(1, -1), w_out.T, bucket_table.T
    )
    received = received.reshape((axis_size * own_heads,) + received.shape[2:])
    dscores, parts = attention_call(bias_vals, received, key_mask, head_dim, rows)
    parts = lax.all_to_all(
        parts.reshape((axis_size, own_heads) + parts.shape[1:]), "heads", split_axis=0, concat_axis=0, tiled=True
    )
    last = 8
    weights = (gain, w_in, w_out.T)
    grad_pairs = backward_call(pair_feats, dscores, pre_act, *weights, 0, rows - last, None)
    parts, grad_pairs = lax.optimization_barrier((parts, grad_pairs))
    dkv_sum, dq_sum = sum_call(parts, head_dim, rows, queries)
    grad_pairs, dkv_sum, dq_sum = lax.optimization_barrier((grad_pairs, dkv_sum, dq_sum))
    dkv_other = other_sum(dkv_sum, "query")
    dq_other = other_sum(dq_sum, "key")
    grad_pairs = backward_call(pair_feats, dscores, pre_act, *weights, rows - last, last, grad_pairs)
    grad_q, grad_k, grad_v = finish_call(dkv_sum, dkv_other, dq_sum, dq_other)
    return (grad_pairs, grad_q, grad_k, grad_v)


def solution(mesh):
    def traced(*args):
        with jax.sharding.use_abstract_mesh(mesh.abstract_mesh):
            return jax.shard_map(
                per_device,
                mesh=mesh,
                in_specs=(
                    P(("query", "heads"), None, "key"),
                    P(("query", "heads"), "key"),
                    P(),
                    P(),
                    P(),
                    P(),
                    P(),
                    P("key"),
                    P("heads", None, "query"),
                    P("heads", None, "key"),
                    P("heads", None, "key"),
                    P("heads", None, "query"),
                    P("heads", None, "query"),
                    P("heads", "query"),
                ),
                out_specs=(
                    P(("query", "heads"), None, "key"),
                    P("heads", None, "query"),
                    P("heads", None, "key"),
                    P("heads", None, "key"),
                ),
                check_vma=False,
            )(*args)

    return traced
```

```python
import functools
import math

import jax
import jax.numpy as jnp
from jax import lax
from jax.experimental import pallas as pl
from jax.experimental.pallas import tpu as pltpu
from jax.sharding import PartitionSpec as P

F32 = jnp.float32
BF16 = jnp.bfloat16
RSQRT2 = 1.0 / math.sqrt(2.0)
EXP2_SCALE = -1.0 / math.log(2.0)
EXP2_SHIFT = math.log2(2.0 / math.sqrt(math.pi))
ROWS = 16
LANES = 128
NT = (((1,), (1,)), ((), ()))
FULL_LIMIT = 60 << 20
BIG_LIMIT = 32 << 20
SMALL_LIMIT = 16 << 20


def low(value):
    return jnp.asarray(value, BF16)


def full_spec(array):
    return pl.BlockSpec(array.shape, lambda *_: (0,) * array.ndim)


def divisor(total, largest):
    return math.gcd(total, largest)


def split_low(values, pieces):
    found = []
    for _ in range(pieces):
        piece = values.astype(BF16).astype(F32)
        found.append(piece)
        values = values - piece
    return found


def as_rows(pieces, count):
    rows = lax.broadcasted_iota(jnp.int32, (count, pieces[0].shape[1]), 0)
    block = jnp.zeros(rows.shape, F32)
    for place, piece in enumerate(pieces):
        block = jnp.where(rows == place, piece, block)
    return block.astype(BF16)


def eye(size):
    rows = lax.broadcasted_iota(jnp.int32, (size, size), 0)
    return jnp.where(rows == lax.broadcasted_iota(jnp.int32, (size, size), 1), 1.0, 0.0).astype(BF16)


def transposed(block):
    return lax.dot_general(eye(block.shape[1]), block, NT, preferred_element_type=F32)


def gain_columns(gain_row):
    chans = gain_row.shape[1]
    total = None
    for piece in split_low(gain_row, 3):
        spread = jnp.broadcast_to(piece, (LANES, chans)).astype(BF16)
        part = lax.dot_general(eye(chans), spread, NT, preferred_element_type=F32)
        total = part if total is None else total + part
    return total


def widen(block, tile):
    return jnp.concatenate([block] * (tile // block.shape[1]), axis=1)


def other_sum(values, name):
    if lax.axis_size(name) == 2:
        return lax.ppermute(values, name, [(0, 1), (1, 0)])
    return lax.psum(values, name) - values


def pack_kernel(k_ref, v_ref, q_ref, dout_ref, out_ref, norm_ref, send_ref, *, rows):
    targets, own_heads, depth, lanes = send_ref.shape
    head_dim = k_ref.shape[1]
    keys = lanes - LANES
    half = LANES // 2
    lane = lax.broadcasted_iota(jnp.int32, (depth, LANES), 1)
    for head in range(own_heads):
        dout = dout_ref[head]
        deltas = jnp.sum(dout.astype(F32) * out_ref[head].astype(F32), axis=0, keepdims=True)
        scalars = as_rows(split_low(norm_ref[head : head + 1, :], 3) + split_low(deltas, 3), depth).astype(F32)
        heads_part = jnp.concatenate([q_ref[head], dout], axis=0).astype(F32)
        for target in range(targets):
            send_ref[target, head, :head_dim, :keys] = k_ref[head]
            send_ref[target, head, head_dim:, :keys] = v_ref[head]
            slab = target * rows // LANES * LANES
            window = (lane >= target * rows - slab) & (lane < target * rows - slab + rows)
            turned = [scalars[:, slab + half : slab + LANES], scalars[:, slab : slab + half]]
            extra = jnp.where(window, heads_part[:, slab : slab + LANES], jnp.concatenate(turned, axis=1))
            send_ref[target, head, :, keys:] = extra.astype(BF16)


def pack_call(k_heads, v_heads, q_heads, dout_heads, out_heads, log_norm, targets, rows):
    own_heads, head_dim, keys = k_heads.shape
    return pl.pallas_call(
        functools.partial(pack_kernel, rows=rows),
        out_shape=jax.ShapeDtypeStruct((targets, own_heads, 2 * head_dim, keys + LANES), BF16),
        compiler_params=pltpu.CompilerParams(vmem_limit_bytes=FULL_LIMIT),
        name="pack_heads",
    )(k_heads, v_heads, q_heads, dout_heads, out_heads, log_norm)


def unit_norm(values):
    centre = values - jnp.mean(values, axis=0, keepdims=True)
    inv_std = lax.rsqrt(jnp.mean(centre * centre, axis=0, keepdims=True) + 1e-05)
    return centre * inv_std, inv_std


def forward_kernel(
    pair_ref, bucket_ref, gain_ref, w_in_ref, b_in_ref, w_out_ref, table_ref, scaled_ref, unit_ref, inv_ref, bias_ref, w_pre,
    w_mix, table, gain, *, group, merge
):
    rows, chans, keys = pair_ref.shape
    heads, buckets = table_ref.shape
    width = merge * keys
    first_row = pl.program_id(0) * rows

    @pl.when(pl.program_id(0) == 0)
    def _():
        stacked = jnp.concatenate([w_in_ref[...], as_rows(split_low(b_in_ref[...], 3), ROWS)], axis=0)
        w_pre[...] = transposed(stacked).astype(BF16)
        w_mix[...] = (w_out_ref[...].astype(F32) * 0.5).astype(BF16)
        place = jnp.where(
            lax.broadcasted_iota(jnp.int32, (buckets, LANES), 0) == lax.broadcasted_iota(jnp.int32, (buckets, LANES), 1),
            1.0,
            0.0,
        ).astype(BF16)
        table[...] = jnp.dot(table_ref[...], place, preferred_element_type=F32)
        gain[...] = gain_columns(gain_ref[...])

    def some_rows(row):
        pairs = jnp.concatenate([pair_ref[row + member] for member in range(merge)], axis=1)
        unit_pairs, inv_std = unit_norm(pairs.astype(F32))
        unit_low = unit_pairs.astype(BF16)
        normed = (unit_pairs * widen(gain[...], width)).astype(BF16)
        ones = jnp.where(lax.broadcasted_iota(jnp.int32, (ROWS, width), 0) < 3, 1.0, 0.0).astype(BF16)
        pre_act = jnp.dot(w_pre[...], jnp.concatenate([normed, ones], axis=0), preferred_element_type=F32)
        scaled = pre_act * RSQRT2
        hidden = (pre_act * (lax.erf(scaled) + 1.0)).astype(BF16)
        scaled_low = scaled.astype(BF16)
        outs = []
        mixed = jnp.dot(w_mix[...], hidden, preferred_element_type=F32)
        for member in range(merge):
            pieces = []
            inv_ref[pl.ds(row + member, 1), :] = inv_std[:, member * keys : (member + 1) * keys]
            id_row = bucket_ref[pl.ds(first_row + row + member, 1), :]
            for part in range(keys // LANES):
                begin = member * keys + part * LANES
                scaled_ref[row + member, part] = scaled_low[:, begin : begin + LANES]
                unit_ref[row + member, part] = unit_low[:, begin : begin + LANES]
                ids = id_row[:, part * LANES : (part + 1) * LANES]
                lookup = jnp.take_along_axis(table[...], jnp.broadcast_to(ids, (heads, LANES)), axis=1)
                pieces.append(mixed[:, begin : begin + LANES] + lookup)
            outs.append(jnp.concatenate(pieces, axis=1))
        return outs

    def step(index, carry):
        outs = []
        for member in range(0, group, merge):
            outs += some_rows(index * group + member)
        size = group * heads
        bias_ref[pl.ds(pl.multiple_of(index * size, size), size), :] = jnp.concatenate(outs, axis=0).astype(BF16)
        return carry

    lax.fori_loop(0, rows // group, step, 0)


def forward_call(pair_feats, bucket_ids, gain, w_in, b_in, w_out, table):
    rows, chans, keys = pair_feats.shape
    heads, hid = w_out.shape
    block = divisor(rows, 8)
    parts = keys // LANES
    return pl.pallas_call(
        functools.partial(forward_kernel, group=block, merge=divisor(block, 2)),
        grid=(rows // block,),
        in_specs=[
            pl.BlockSpec((block, chans, keys), lambda i: (i, 0, 0)),
            full_spec(bucket_ids),
            full_spec(gain),
            full_spec(w_in),
            full_spec(b_in),
            full_spec(w_out),
            full_spec(table),
        ],
        out_specs=[
            pl.BlockSpec((block, parts, hid, LANES), lambda i: (i, 0, 0, 0)),
            pl.BlockSpec((block, parts, chans, LANES), lambda i: (i, 0, 0, 0)),
            pl.BlockSpec((block, keys), lambda i: (i, 0)),
            pl.BlockSpec((block * heads, keys), lambda i: (i, 0)),
        ],
        out_shape=[
            jax.ShapeDtypeStruct((rows, parts, hid, LANES), BF16),
            jax.ShapeDtypeStruct((rows, parts, chans, LANES), BF16),
            jax.ShapeDtypeStruct((rows, keys), F32),
            jax.ShapeDtypeStruct((rows * heads, keys), BF16),
        ],
        scratch_shapes=[
            pltpu.VMEM((hid, chans + ROWS), BF16),
            pltpu.VMEM((heads, hid), BF16),
            pltpu.VMEM((heads, LANES), F32),
            pltpu.VMEM((chans, LANES), F32),
        ],
        compiler_params=pltpu.CompilerParams(vmem_limit_bytes=FULL_LIMIT),
        cost_estimate=pl.CostEstimate(
            flops=2 * rows * keys * hid * 256,
            bytes_accessed=2 * rows * keys * (hid + chans),
            transcendentals=2 * rows * keys * hid,
        ),
        name="pair_forward",
    )(pair_feats, bucket_ids, gain, w_in, b_in, w_out, table)


def attention_kernel(
    bias_ref, kv_ref, aux_ref, mask_ref, ds_ref, part_ref, q_rows, d_rows, q_cols, d_cols, norm_ref, delta_ref,
    dq_acc, *, head_dim, rows
):
    heads = kv_ref.shape[0]
    tile = bias_ref.shape[1]
    width = heads * head_dim
    flat = rows * heads
    scale = 1.0 / math.sqrt(head_dim)
    step = pl.program_id(0)
    cols = pl.ds(pl.multiple_of(step * tile, tile), tile)
    offset = lax.rem(lax.axis_index("heads") * rows, LANES)
    scalar_offset = lax.rem(offset + LANES // 2, LANES)

    def spread_matrix():
        lane = lax.broadcasted_iota(jnp.int32, (flat, LANES), 1)
        return lane == lax.broadcasted_iota(jnp.int32, (flat, LANES), 0) // heads + offset

    def own_columns():
        return (
            lax.broadcasted_iota(jnp.int32, (width, flat), 1) % heads
            == lax.broadcasted_iota(jnp.int32, (width, flat), 0) // head_dim
        )

    @pl.when(step == 0)
    def _():
        spread_low = jnp.where(spread_matrix(), 1.0, 0.0).astype(BF16)
        own_rows = (
            lax.broadcasted_iota(jnp.int32, (flat, width), 0) % heads
            == lax.broadcasted_iota(jnp.int32, (flat, width), 1) // head_dim
        )
        own_cols = own_columns()
        for begin, by_rows, by_cols in ((0, q_rows, q_cols), (head_dim, d_rows, d_cols)):
            block = aux_ref[:, begin : begin + head_dim, :].reshape(width, LANES)
            spread = lax.dot_general(spread_low, block, NT, preferred_element_type=F32)
            by_rows[...] = jnp.where(own_rows, spread, 0.0).astype(BF16)
            spread = lax.dot_general(block, spread_low, NT, preferred_element_type=F32)
            by_cols[...] = jnp.where(own_cols, spread, 0.0).astype(BF16)
        tail = aux_ref[:, :ROWS, :].astype(F32)
        lane = lax.broadcasted_iota(jnp.int32, (rows, heads, LANES), 2)
        own_lane = lane == lax.broadcasted_iota(jnp.int32, (rows, heads, LANES), 0) + scalar_offset
        for begin, target in ((0, norm_ref), (3, delta_ref)):
            pieces = tail[:, begin, :] + tail[:, begin + 1, :] + tail[:, begin + 2, :]
            column = jnp.sum(jnp.where(own_lane, pieces[None], 0.0), axis=2, keepdims=True)
            target[...] = jnp.broadcast_to(column.reshape(flat, 1), target.shape)
        dq_acc[...] = jnp.zeros_like(dq_acc)

    norm = widen(norm_ref[...], tile)
    delta = widen(delta_ref[...], tile)
    keys = kv_ref[:, :head_dim, :].reshape(width, tile)
    values = kv_ref[:, head_dim:, :].reshape(width, tile)
    scores = jnp.dot(q_rows[...], keys, preferred_element_type=F32) * scale + bias_ref[...].astype(F32)
    probs = jnp.where(mask_ref[...] == 1, jnp.exp(scores - norm), 0.0)
    dprobs = jnp.dot(d_rows[...], values, preferred_element_type=F32)
    dscores = (probs * (dprobs - delta)).astype(BF16)
    ds_ref[...] = dscores
    dk_part = jnp.dot(q_cols[...], dscores, preferred_element_type=F32)
    dv_part = jnp.dot(d_cols[...], probs.astype(BF16), preferred_element_type=F32)
    part_ref[:, :head_dim, cols] = dk_part.reshape(heads, head_dim, tile).astype(BF16)
    part_ref[:, head_dim : 2 * head_dim, cols] = dv_part.reshape(heads, head_dim, tile).astype(BF16)
    dq_acc[...] += lax.dot_general(keys, dscores, NT, preferred_element_type=F32)

    @pl.when(step == pl.num_programs(0) - 1)
    def _():
        spread_low = jnp.where(spread_matrix(), 1.0, 0.0).astype(BF16)
        total = None
        for piece in split_low(jnp.where(own_columns(), dq_acc[...], 0.0), 3):
            part = jnp.dot(piece.astype(BF16), spread_low, preferred_element_type=F32)
            total = part if total is None else total + part
        high, rest = split_low(total, 2)
        keys_end = part_ref.shape[2] - LANES
        part_ref[:, :head_dim, keys_end:] = high.astype(BF16).reshape(heads, head_dim, LANES)
        part_ref[:, head_dim:, keys_end:] = rest.astype(BF16).reshape(heads, head_dim, LANES)


def attention_call(bias, received, key_mask, head_dim, rows):
    flat, keys = bias.shape
    heads, depth, _ = received.shape
    width = heads * head_dim
    tile = divisor(keys, 256)
    return pl.pallas_call(
        functools.partial(attention_kernel, head_dim=head_dim, rows=rows),
        grid=(keys // tile,),
        in_specs=[
            pl.BlockSpec((flat, tile), lambda i: (0, i)),
            pl.BlockSpec((heads, 2 * head_dim, tile), lambda i: (0, 0, i)),
            pl.BlockSpec((heads, depth, LANES), lambda i: (0, 0, keys // LANES)),
            pl.BlockSpec((1, tile), lambda i: (0, i)),
        ],
        out_specs=[
            pl.BlockSpec((flat, tile), lambda i: (0, i)),
            pl.BlockSpec((heads, depth, keys + LANES), lambda i: (0, 0, 0)),
        ],
        out_shape=[
            jax.ShapeDtypeStruct((flat, keys), BF16),
            jax.ShapeDtypeStruct((heads, depth, keys + LANES), BF16),
        ],
        scratch_shapes=[
            pltpu.VMEM((flat, width), BF16),
            pltpu.VMEM((flat, width), BF16),
            pltpu.VMEM((width, flat), BF16),
            pltpu.VMEM((width, flat), BF16),
            pltpu.VMEM((flat, LANES), F32),
            pltpu.VMEM((flat, LANES), F32),
            pltpu.VMEM((width, flat), F32),
        ],
        compiler_params=pltpu.CompilerParams(vmem_limit_bytes=BIG_LIMIT),
        cost_estimate=pl.CostEstimate(
            flops=10 * flat * keys * width, bytes_accessed=8 * flat * keys, transcendentals=flat * keys
        ),
        name="pair_attention",
    )(bias, received, received, key_mask.reshape(1, keys))


def backward_kernel(unit_ref, inv_ref, ds_ref, scaled_ref, gain_ref, w_in_ref, w_out_ref, *rest, group, merge):
    out_ref, w_back, gain = rest[-3:]
    rows, parts, chans, _ = unit_ref.shape
    heads = w_out_ref.shape[0]
    keys = parts * LANES

    @pl.when(pl.program_id(0) == 0)
    def _():
        w_back[...] = (transposed(w_out_ref[...]) * 0.5).astype(BF16)
        gain[...] = gain_columns(gain_ref[...])

    def step(index, carry):
        size = group * heads
        dscores = ds_ref[pl.ds(pl.multiple_of(index * size, size), size), :]
        for begin in range(0, group, merge):
            members = range(begin, begin + merge)
            tiles = [(index * group + member, part) for member in members for part in range(parts)]
            unit_pairs = jnp.concatenate([unit_ref[row, part] for row, part in tiles], axis=1).astype(F32)
            scaled = jnp.concatenate([scaled_ref[row, part] for row, part in tiles], axis=1)
            inv_std = jnp.concatenate([inv_ref[pl.ds(index * group + member, 1), :] for member in members], axis=1)
            own = [dscores[member * heads : (member + 1) * heads] for member in members]
            density2 = jnp.exp2(scaled * scaled * low(EXP2_SCALE) + low(EXP2_SHIFT))
            slope = lax.erf(scaled) + low(1.0) + scaled * density2
            dhidden = jnp.dot(w_back[...], jnp.concatenate(own, axis=1), preferred_element_type=F32)
            dpre = dhidden.astype(BF16) * slope
            dunit = jnp.dot(w_in_ref[...], dpre, preferred_element_type=F32) * widen(gain[...], keys * merge)
            first_mean = jnp.mean(dunit, axis=0, keepdims=True)
            second_mean = jnp.mean(dunit * unit_pairs, axis=0, keepdims=True)
            grad = (inv_std * (dunit - first_mean - unit_pairs * second_mean)).astype(BF16)
            for place, member in enumerate(members):
                out_ref[index * group + member] = grad[:, place * keys : (place + 1) * keys]
        return carry

    lax.fori_loop(0, rows // group, step, 0)


def backward_call(unit_pairs, inv_std, dscores, scaled, gain, w_in, w_out, begin, count, previous):
    rows, parts, chans, _ = unit_pairs.shape
    keys = parts * LANES
    heads, hid = w_out.shape
    block = divisor(math.gcd(begin, count), 8)
    first = begin // block
    operands = [unit_pairs, inv_std, dscores, scaled, gain, w_in, w_out]
    in_specs = [
        pl.BlockSpec((block, parts, chans, LANES), lambda i: (i + first, 0, 0, 0)),
        pl.BlockSpec((block, keys), lambda i: (i + first, 0)),
        pl.BlockSpec((block * heads, keys), lambda i: (i + first, 0)),
        pl.BlockSpec((block, parts, hid, LANES), lambda i: (i + first, 0, 0, 0)),
        full_spec(gain),
        full_spec(w_in),
        full_spec(w_out),
    ]
    aliases = {}
    if previous is not None:
        aliases = {len(operands): 0}
        operands.append(previous)
        in_specs.append(pl.BlockSpec(memory_space=pl.ANY))
    return pl.pallas_call(
        functools.partial(backward_kernel, group=block, merge=divisor(block, 2)),
        grid=(count // block,),
        in_specs=in_specs,
        out_specs=pl.BlockSpec((block, chans, keys), lambda i: (i + first, 0, 0)),
        out_shape=jax.ShapeDtypeStruct((rows, chans, keys), BF16),
        scratch_shapes=[pltpu.VMEM((hid, heads), BF16), pltpu.VMEM((chans, LANES), F32)],
        input_output_aliases=aliases,
        compiler_params=pltpu.CompilerParams(vmem_limit_bytes=FULL_LIMIT),
        cost_estimate=pl.CostEstimate(
            flops=2 * count * keys * hid * 256,
            bytes_accessed=2 * count * keys * (hid + 2 * chans),
            transcendentals=0,
        ),
        name="pair_backward",
    )(*operands)


def sum_kernel(part_ref, dkv_ref, dq_ref, *, head_dim, rows):
    sources, own_heads, _, lanes = part_ref.shape
    keys = lanes - LANES
    for head in range(own_heads):
        total = part_ref[0, head, :, :keys].astype(F32)
        for source in range(1, sources):
            total = total + part_ref[source, head, :, :keys].astype(F32)
        dkv_ref[head] = total
        dq_ref[head] = jnp.zeros(dq_ref.shape[1:], F32)
        for source in range(sources):
            slab = source * rows // LANES * LANES
            piece = part_ref[source, head, :, keys:].astype(F32)
            dq_ref[head, :, slab : slab + LANES] += piece[:head_dim] + piece[head_dim:]


def sum_call(parts, head_dim, rows, queries):
    _, own_heads, _, lanes = parts.shape
    return pl.pallas_call(
        functools.partial(sum_kernel, head_dim=head_dim, rows=rows),
        out_shape=[
            jax.ShapeDtypeStruct((own_heads, 2 * head_dim, lanes - LANES), F32),
            jax.ShapeDtypeStruct((own_heads, head_dim, queries), F32),
        ],
        compiler_params=pltpu.CompilerParams(vmem_limit_bytes=SMALL_LIMIT),
        name="sum_sources",
    )(parts)


def finish_kernel(dkv_ref, dkv_other, dq_ref, dq_other, grad_q, grad_k, grad_v, *, head_dim):
    scale = 1.0 / math.sqrt(head_dim)
    total = dkv_ref[...] + dkv_other[...]
    grad_q[...] = ((dq_ref[...] + dq_other[...]) * scale).astype(BF16)
    grad_k[...] = (total[:, :head_dim, :] * scale).astype(BF16)
    grad_v[...] = total[:, head_dim:, :].astype(BF16)


def finish_call(dkv, dkv_other, dq, dq_other):
    own_heads, head_dim, queries = dq.shape
    keys = dkv.shape[2]
    return pl.pallas_call(
        functools.partial(finish_kernel, head_dim=head_dim),
        out_shape=[
            jax.ShapeDtypeStruct((own_heads, head_dim, queries), BF16),
            jax.ShapeDtypeStruct((own_heads, head_dim, keys), BF16),
            jax.ShapeDtypeStruct((own_heads, head_dim, keys), BF16),
        ],
        compiler_params=pltpu.CompilerParams(vmem_limit_bytes=SMALL_LIMIT),
        name="finish",
    )(dkv, dkv_other, dq, dq_other)


def per_device(
    pair_feats,
    bucket_ids,
    ln_gain,
    w_in,
    b_in,
    w_out,
    bucket_table,
    key_mask,
    q_heads,
    k_heads,
    v_heads,
    out_heads,
    dout_heads,
    log_norm,
):
    axis_size = lax.axis_size("heads")
    own_heads, head_dim, queries = q_heads.shape
    rows = pair_feats.shape[0]
    gain = ln_gain.reshape(1, -1)

    packed = pack_call(k_heads, v_heads, q_heads, dout_heads, out_heads, log_norm, axis_size, rows)
    received = lax.all_to_all(packed, "heads", split_axis=0, concat_axis=0, tiled=True)
    scaled, unit_pairs, inv_std, bias_vals = forward_call(
        pair_feats, bucket_ids, gain, w_in, b_in.reshape(1, -1), w_out.T, bucket_table.T
    )
    received = received.reshape((axis_size * own_heads,) + received.shape[2:])
    dscores, parts = attention_call(bias_vals, received, key_mask, head_dim, rows)
    parts = lax.all_to_all(
        parts.reshape((axis_size, own_heads) + parts.shape[1:]), "heads", split_axis=0, concat_axis=0, tiled=True
    )
    last = 8
    weights = (gain, w_in, w_out.T)
    grad_pairs = backward_call(unit_pairs, inv_std, dscores, scaled, *weights, 0, rows - last, None)
    parts, grad_pairs = lax.optimization_barrier((parts, grad_pairs))
    dkv_sum, dq_sum = sum_call(parts, head_dim, rows, queries)
    grad_pairs, dkv_sum, dq_sum = lax.optimization_barrier((grad_pairs, dkv_sum, dq_sum))
    dkv_other = other_sum(dkv_sum, "query")
    dq_other = other_sum(dq_sum, "key")
    grad_pairs = backward_call(unit_pairs, inv_std, dscores, scaled, *weights, rows - last, last, grad_pairs)
    grad_q, grad_k, grad_v = finish_call(dkv_sum, dkv_other, dq_sum, dq_other)
    return (grad_pairs, grad_q, grad_k, grad_v)


def solution(mesh):
    def traced(*args):
        with jax.sharding.use_abstract_mesh(mesh.abstract_mesh):
            return jax.shard_map(
                per_device,
                mesh=mesh,
                in_specs=(
                    P(("query", "heads"), None, "key"),
                    P(("query", "heads"), "key"),
                    P(),
                    P(),
                    P(),
                    P(),
                    P(),
                    P("key"),
                    P("heads", None, "query"),
                    P("heads", None, "key"),
                    P("heads", None, "key"),
                    P("heads", None, "query"),
                    P("heads", None, "query"),
                    P("heads", "query"),
                ),
                out_specs=(
                    P(("query", "heads"), None, "key"),
                    P("heads", None, "query"),
                    P("heads", None, "key"),
                    P("heads", None, "key"),
                ),
                check_vma=False,
            )(*args)

    return traced
```

```python
import functools
import math

import jax
import jax.numpy as jnp
from jax import lax
from jax.experimental import pallas as pl
from jax.experimental.pallas import tpu as pltpu
from jax.sharding import PartitionSpec as P

F32 = jnp.float32
BF16 = jnp.bfloat16
RSQRT2 = 1.0 / math.sqrt(2.0)
EXP2_SCALE = -1.0 / math.log(2.0)
EXP2_SHIFT = math.log2(2.0 / math.sqrt(math.pi))
ROWS = 16
LANES = 128
READY = 2
NT = (((1,), (1,)), ((), ()))
FULL_LIMIT = 60 << 20
BIG_LIMIT = 32 << 20
SMALL_LIMIT = 16 << 20


def low(value):
    return jnp.asarray(value, BF16)


def full_spec(array):
    return pl.BlockSpec(array.shape, lambda *_: (0,) * array.ndim)


def divisor(total, largest):
    return math.gcd(total, largest)


def split_low(values, pieces):
    found = []
    for _ in range(pieces):
        piece = values.astype(BF16).astype(F32)
        found.append(piece)
        values = values - piece
    return found


def as_rows(pieces, count):
    rows = lax.broadcasted_iota(jnp.int32, (count, pieces[0].shape[1]), 0)
    block = jnp.zeros(rows.shape, F32)
    for place, piece in enumerate(pieces):
        block = jnp.where(rows == place, piece, block)
    return block.astype(BF16)


def eye(size):
    rows = lax.broadcasted_iota(jnp.int32, (size, size), 0)
    return jnp.where(rows == lax.broadcasted_iota(jnp.int32, (size, size), 1), 1.0, 0.0).astype(BF16)


def transposed(block):
    return lax.dot_general(eye(block.shape[1]), block, NT, preferred_element_type=F32)


def gain_columns(gain_row):
    chans = gain_row.shape[1]
    total = None
    for piece in split_low(gain_row, 3):
        spread = jnp.broadcast_to(piece, (LANES, chans)).astype(BF16)
        part = lax.dot_general(eye(chans), spread, NT, preferred_element_type=F32)
        total = part if total is None else total + part
    return total


def widen(block, tile):
    return jnp.concatenate([block] * (tile // block.shape[1]), axis=1)


def other_sum(values, name):
    if lax.axis_size(name) == 2:
        return lax.ppermute(values, name, [(0, 1), (1, 0)])
    return lax.psum(values, name) - values


def pack_kernel(k_ref, v_ref, q_ref, dout_ref, out_ref, norm_ref, send_ref, *, rows):
    targets, own_heads, depth, lanes = send_ref.shape
    head_dim = k_ref.shape[1]
    keys = lanes - LANES
    half = LANES // 2
    lane = lax.broadcasted_iota(jnp.int32, (depth, LANES), 1)
    for head in range(own_heads):
        dout = dout_ref[head]
        deltas = jnp.sum(dout.astype(F32) * out_ref[head].astype(F32), axis=0, keepdims=True)
        scalars = as_rows(split_low(norm_ref[head : head + 1, :], 3) + split_low(deltas, 3), depth).astype(F32)
        heads_part = jnp.concatenate([q_ref[head], dout], axis=0).astype(F32)
        for target in range(targets):
            send_ref[target, head, :head_dim, :keys] = k_ref[head]
            send_ref[target, head, head_dim:, :keys] = v_ref[head]
            slab = target * rows // LANES * LANES
            window = (lane >= target * rows - slab) & (lane < target * rows - slab + rows)
            turned = [scalars[:, slab + half : slab + LANES], scalars[:, slab : slab + half]]
            extra = jnp.where(window, heads_part[:, slab : slab + LANES], jnp.concatenate(turned, axis=1))
            send_ref[target, head, :, keys:] = extra.astype(BF16)


def pack_call(k_heads, v_heads, q_heads, dout_heads, out_heads, log_norm, targets, rows):
    own_heads, head_dim, keys = k_heads.shape
    return pl.pallas_call(
        functools.partial(pack_kernel, rows=rows),
        out_shape=jax.ShapeDtypeStruct((targets, own_heads, 2 * head_dim, keys + LANES), BF16),
        compiler_params=pltpu.CompilerParams(vmem_limit_bytes=FULL_LIMIT),
        name="pack_heads",
    )(k_heads, v_heads, q_heads, dout_heads, out_heads, log_norm)


def slope_of(scaled, cdf2):
    density2 = jnp.exp2(scaled * scaled * low(EXP2_SCALE) + low(EXP2_SHIFT))
    return cdf2 + scaled * density2


def unit_norm(values):
    centre = values - jnp.mean(values, axis=0, keepdims=True)
    inv_std = lax.rsqrt(jnp.mean(centre * centre, axis=0, keepdims=True) + 1e-05)
    return centre * inv_std, inv_std


def forward_kernel(
    pair_ref, bucket_ref, gain_ref, w_in_ref, b_in_ref, w_out_ref, table_ref, saved_ref, unit_ref, inv_ref, bias_ref, w_pre,
    w_mix, table, gain, *, group, merge, ready
):
    rows, chans, keys = pair_ref.shape
    heads, buckets = table_ref.shape
    width = merge * keys
    first_row = pl.program_id(0) * rows

    @pl.when(pl.program_id(0) == 0)
    def _():
        stacked = jnp.concatenate([w_in_ref[...], as_rows(split_low(b_in_ref[...], 3), ROWS)], axis=0)
        w_pre[...] = transposed(stacked).astype(BF16)
        w_mix[...] = (w_out_ref[...].astype(F32) * 0.5).astype(BF16)
        place = jnp.where(
            lax.broadcasted_iota(jnp.int32, (buckets, LANES), 0) == lax.broadcasted_iota(jnp.int32, (buckets, LANES), 1),
            1.0,
            0.0,
        ).astype(BF16)
        table[...] = jnp.dot(table_ref[...], place, preferred_element_type=F32)
        gain[...] = gain_columns(gain_ref[...])

    def some_rows(row, with_slope):
        pairs = jnp.concatenate([pair_ref[row + member] for member in range(merge)], axis=1)
        unit_pairs, inv_std = unit_norm(pairs.astype(F32))
        unit_low = unit_pairs.astype(BF16)
        normed = (unit_pairs * widen(gain[...], width)).astype(BF16)
        ones = jnp.where(lax.broadcasted_iota(jnp.int32, (ROWS, width), 0) < 3, 1.0, 0.0).astype(BF16)
        pre_act = jnp.dot(w_pre[...], jnp.concatenate([normed, ones], axis=0), preferred_element_type=F32)
        scaled = pre_act * RSQRT2
        cdf2 = lax.erf(scaled) + 1.0
        hidden = (pre_act * cdf2).astype(BF16)
        saved = scaled.astype(BF16)
        if with_slope:
            saved = slope_of(saved, cdf2.astype(BF16))
        outs = []
        mixed = jnp.dot(w_mix[...], hidden, preferred_element_type=F32)
        for member in range(merge):
            pieces = []
            inv_ref[pl.ds(row + member, 1), :] = inv_std[:, member * keys : (member + 1) * keys]
            id_row = bucket_ref[pl.ds(first_row + row + member, 1), :]
            for part in range(keys // LANES):
                begin = member * keys + part * LANES
                saved_ref[row + member, part] = saved[:, begin : begin + LANES]
                unit_ref[row + member, part] = unit_low[:, begin : begin + LANES]
                ids = id_row[:, part * LANES : (part + 1) * LANES]
                lookup = jnp.take_along_axis(table[...], jnp.broadcast_to(ids, (heads, LANES)), axis=1)
                pieces.append(mixed[:, begin : begin + LANES] + lookup)
            outs.append(jnp.concatenate(pieces, axis=1))
        return outs

    def step(index, carry):
        outs = []
        for member in range(0, group, merge):
            outs += some_rows(index * group + member, member < ready)
        size = group * heads
        bias_ref[pl.ds(pl.multiple_of(index * size, size), size), :] = jnp.concatenate(outs, axis=0).astype(BF16)
        return carry

    lax.fori_loop(0, rows // group, step, 0)


def forward_call(pair_feats, bucket_ids, gain, w_in, b_in, w_out, table):
    rows, chans, keys = pair_feats.shape
    heads, hid = w_out.shape
    block = divisor(rows, 8)
    parts = keys // LANES
    return pl.pallas_call(
        functools.partial(forward_kernel, group=block, merge=divisor(block, 2), ready=READY),
        grid=(rows // block,),
        in_specs=[
            pl.BlockSpec((block, chans, keys), lambda i: (i, 0, 0)),
            full_spec(bucket_ids),
            full_spec(gain),
            full_spec(w_in),
            full_spec(b_in),
            full_spec(w_out),
            full_spec(table),
        ],
        out_specs=[
            pl.BlockSpec((block, parts, hid, LANES), lambda i: (i, 0, 0, 0)),
            pl.BlockSpec((block, parts, chans, LANES), lambda i: (i, 0, 0, 0)),
            pl.BlockSpec((block, keys), lambda i: (i, 0)),
            pl.BlockSpec((block * heads, keys), lambda i: (i, 0)),
        ],
        out_shape=[
            jax.ShapeDtypeStruct((rows, parts, hid, LANES), BF16),
            jax.ShapeDtypeStruct((rows, parts, chans, LANES), BF16),
            jax.ShapeDtypeStruct((rows, keys), F32),
            jax.ShapeDtypeStruct((rows * heads, keys), BF16),
        ],
        scratch_shapes=[
            pltpu.VMEM((hid, chans + ROWS), BF16),
            pltpu.VMEM((heads, hid), BF16),
            pltpu.VMEM((heads, LANES), F32),
            pltpu.VMEM((chans, LANES), F32),
        ],
        compiler_params=pltpu.CompilerParams(vmem_limit_bytes=FULL_LIMIT),
        cost_estimate=pl.CostEstimate(
            flops=2 * rows * keys * hid * 256,
            bytes_accessed=2 * rows * keys * (hid + chans),
            transcendentals=2 * rows * keys * hid,
        ),
        name="pair_forward",
    )(pair_feats, bucket_ids, gain, w_in, b_in, w_out, table)


def attention_kernel(
    bias_ref, kv_ref, aux_ref, mask_ref, ds_ref, part_ref, q_rows, d_rows, q_cols, d_cols, norm_ref, delta_ref,
    dq_acc, *, head_dim, rows
):
    heads = kv_ref.shape[0]
    tile = bias_ref.shape[1]
    width = heads * head_dim
    flat = rows * heads
    scale = 1.0 / math.sqrt(head_dim)
    step = pl.program_id(0)
    cols = pl.ds(pl.multiple_of(step * tile, tile), tile)
    offset = lax.rem(lax.axis_index("heads") * rows, LANES)
    scalar_offset = lax.rem(offset + LANES // 2, LANES)

    def spread_matrix():
        lane = lax.broadcasted_iota(jnp.int32, (flat, LANES), 1)
        return lane == lax.broadcasted_iota(jnp.int32, (flat, LANES), 0) // heads + offset

    def own_columns():
        return (
            lax.broadcasted_iota(jnp.int32, (width, flat), 1) % heads
            == lax.broadcasted_iota(jnp.int32, (width, flat), 0) // head_dim
        )

    @pl.when(step == 0)
    def _():
        spread_low = jnp.where(spread_matrix(), 1.0, 0.0).astype(BF16)
        own_rows = (
            lax.broadcasted_iota(jnp.int32, (flat, width), 0) % heads
            == lax.broadcasted_iota(jnp.int32, (flat, width), 1) // head_dim
        )
        own_cols = own_columns()
        for begin, by_rows, by_cols in ((0, q_rows, q_cols), (head_dim, d_rows, d_cols)):
            block = aux_ref[:, begin : begin + head_dim, :].reshape(width, LANES)
            spread = lax.dot_general(spread_low, block, NT, preferred_element_type=F32)
            by_rows[...] = jnp.where(own_rows, spread, 0.0).astype(BF16)
            spread = lax.dot_general(block, spread_low, NT, preferred_element_type=F32)
            by_cols[...] = jnp.where(own_cols, spread, 0.0).astype(BF16)
        tail = aux_ref[:, :ROWS, :].astype(F32)
        lane = lax.broadcasted_iota(jnp.int32, (rows, heads, LANES), 2)
        own_lane = lane == lax.broadcasted_iota(jnp.int32, (rows, heads, LANES), 0) + scalar_offset
        for begin, target in ((0, norm_ref), (3, delta_ref)):
            pieces = tail[:, begin, :] + tail[:, begin + 1, :] + tail[:, begin + 2, :]
            column = jnp.sum(jnp.where(own_lane, pieces[None], 0.0), axis=2, keepdims=True)
            target[...] = jnp.broadcast_to(column.reshape(flat, 1), target.shape)
        dq_acc[...] = jnp.zeros_like(dq_acc)

    norm = widen(norm_ref[...], tile)
    delta = widen(delta_ref[...], tile)
    keys = kv_ref[:, :head_dim, :].reshape(width, tile)
    values = kv_ref[:, head_dim:, :].reshape(width, tile)
    scores = jnp.dot(q_rows[...], keys, preferred_element_type=F32) * scale + bias_ref[...].astype(F32)
    probs = jnp.where(mask_ref[...] == 1, jnp.exp(scores - norm), 0.0)
    dprobs = jnp.dot(d_rows[...], values, preferred_element_type=F32)
    dscores = (probs * (dprobs - delta)).astype(BF16)
    ds_ref[...] = dscores
    dk_part = jnp.dot(q_cols[...], dscores, preferred_element_type=F32)
    dv_part = jnp.dot(d_cols[...], probs.astype(BF16), preferred_element_type=F32)
    part_ref[:, :head_dim, cols] = dk_part.reshape(heads, head_dim, tile).astype(BF16)
    part_ref[:, head_dim : 2 * head_dim, cols] = dv_part.reshape(heads, head_dim, tile).astype(BF16)
    dq_acc[...] += lax.dot_general(keys, dscores, NT, preferred_element_type=F32)

    @pl.when(step == pl.num_programs(0) - 1)
    def _():
        spread_low = jnp.where(spread_matrix(), 1.0, 0.0).astype(BF16)
        total = None
        for piece in split_low(jnp.where(own_columns(), dq_acc[...], 0.0), 3):
            part = jnp.dot(piece.astype(BF16), spread_low, preferred_element_type=F32)
            total = part if total is None else total + part
        high, rest = split_low(total, 2)
        keys_end = part_ref.shape[2] - LANES
        part_ref[:, :head_dim, keys_end:] = high.astype(BF16).reshape(heads, head_dim, LANES)
        part_ref[:, head_dim:, keys_end:] = rest.astype(BF16).reshape(heads, head_dim, LANES)


def attention_call(bias, received, key_mask, head_dim, rows):
    flat, keys = bias.shape
    heads, depth, _ = received.shape
    width = heads * head_dim
    tile = divisor(keys, 256)
    return pl.pallas_call(
        functools.partial(attention_kernel, head_dim=head_dim, rows=rows),
        grid=(keys // tile,),
        in_specs=[
            pl.BlockSpec((flat, tile), lambda i: (0, i)),
            pl.BlockSpec((heads, 2 * head_dim, tile), lambda i: (0, 0, i)),
            pl.BlockSpec((heads, depth, LANES), lambda i: (0, 0, keys // LANES)),
            pl.BlockSpec((1, tile), lambda i: (0, i)),
        ],
        out_specs=[
            pl.BlockSpec((flat, tile), lambda i: (0, i)),
            pl.BlockSpec((heads, depth, keys + LANES), lambda i: (0, 0, 0)),
        ],
        out_shape=[
            pltpu.HBM((flat, keys), BF16),
            jax.ShapeDtypeStruct((heads, depth, keys + LANES), BF16),
        ],
        scratch_shapes=[
            pltpu.VMEM((flat, width), BF16),
            pltpu.VMEM((flat, width), BF16),
            pltpu.VMEM((width, flat), BF16),
            pltpu.VMEM((width, flat), BF16),
            pltpu.VMEM((flat, LANES), F32),
            pltpu.VMEM((flat, LANES), F32),
            pltpu.VMEM((width, flat), F32),
        ],
        compiler_params=pltpu.CompilerParams(vmem_limit_bytes=BIG_LIMIT),
        cost_estimate=pl.CostEstimate(
            flops=10 * flat * keys * width, bytes_accessed=8 * flat * keys, transcendentals=flat * keys
        ),
        name="pair_attention",
    )(pltpu.with_memory_space_constraint(bias, pltpu.HBM), received, received, key_mask.reshape(1, keys))


def backward_kernel(unit_ref, inv_ref, ds_ref, saved_ref, gain_ref, w_in_ref, w_out_ref, *rest, group, merge, ready):
    out_ref, w_back, gain = rest[-3:]
    rows, parts, chans, _ = unit_ref.shape
    heads = w_out_ref.shape[0]
    keys = parts * LANES

    @pl.when(pl.program_id(0) == 0)
    def _():
        w_back[...] = (transposed(w_out_ref[...]) * 0.5).astype(BF16)
        gain[...] = gain_columns(gain_ref[...])

    def step(index, carry):
        size = group * heads
        dscores = ds_ref[pl.ds(pl.multiple_of(index * size, size), size), :]
        for begin in range(0, group, merge):
            members = range(begin, begin + merge)
            tiles = [(index * group + member, part) for member in members for part in range(parts)]
            unit_pairs = jnp.concatenate([unit_ref[row, part] for row, part in tiles], axis=1).astype(F32)
            saved = jnp.concatenate([saved_ref[row, part] for row, part in tiles], axis=1)
            inv_std = jnp.concatenate([inv_ref[pl.ds(index * group + member, 1), :] for member in members], axis=1)
            own = [dscores[member * heads : (member + 1) * heads] for member in members]
            slope = saved if begin < ready else slope_of(saved, lax.erf(saved) + low(1.0))
            dhidden = jnp.dot(w_back[...], jnp.concatenate(own, axis=1), preferred_element_type=F32)
            dpre = dhidden.astype(BF16) * slope
            dunit = jnp.dot(w_in_ref[...], dpre, preferred_element_type=F32) * widen(gain[...], keys * merge)
            first_mean = jnp.mean(dunit, axis=0, keepdims=True)
            second_mean = jnp.mean(dunit * unit_pairs, axis=0, keepdims=True)
            grad = (inv_std * (dunit - first_mean - unit_pairs * second_mean)).astype(BF16)
            for place, member in enumerate(members):
                out_ref[index * group + member] = grad[:, place * keys : (place + 1) * keys]
        return carry

    lax.fori_loop(0, rows // group, step, 0)


def backward_call(unit_pairs, inv_std, dscores, saved, gain, w_in, w_out, begin, count, previous):
    rows, parts, chans, _ = unit_pairs.shape
    keys = parts * LANES
    heads, hid = w_out.shape
    block = divisor(math.gcd(begin, count), 8)
    first = begin // block
    operands = [unit_pairs, inv_std, dscores, saved, gain, w_in, w_out]
    in_specs = [
        pl.BlockSpec((block, parts, chans, LANES), lambda i: (i + first, 0, 0, 0)),
        pl.BlockSpec((block, keys), lambda i: (i + first, 0)),
        pl.BlockSpec((block * heads, keys), lambda i: (i + first, 0)),
        pl.BlockSpec((block, parts, hid, LANES), lambda i: (i + first, 0, 0, 0)),
        full_spec(gain),
        full_spec(w_in),
        full_spec(w_out),
    ]
    aliases = {}
    if previous is not None:
        aliases = {len(operands): 0}
        operands.append(previous)
        in_specs.append(pl.BlockSpec(memory_space=pl.ANY))
    return pl.pallas_call(
        functools.partial(backward_kernel, group=block, merge=divisor(block, 2), ready=READY),
        grid=(count // block,),
        in_specs=in_specs,
        out_specs=pl.BlockSpec((block, chans, keys), lambda i: (i + first, 0, 0)),
        out_shape=jax.ShapeDtypeStruct((rows, chans, keys), BF16),
        scratch_shapes=[pltpu.VMEM((hid, heads), BF16), pltpu.VMEM((chans, LANES), F32)],
        input_output_aliases=aliases,
        compiler_params=pltpu.CompilerParams(vmem_limit_bytes=FULL_LIMIT),
        cost_estimate=pl.CostEstimate(
            flops=2 * count * keys * hid * 256,
            bytes_accessed=2 * count * keys * (hid + 2 * chans),
            transcendentals=0,
        ),
        name="pair_backward",
    )(*operands)


def sum_kernel(part_ref, dkv_ref, dq_ref, *, head_dim, rows):
    sources, own_heads, _, lanes = part_ref.shape
    keys = lanes - LANES
    for head in range(own_heads):
        total = part_ref[0, head, :, :keys].astype(F32)
        for source in range(1, sources):
            total = total + part_ref[source, head, :, :keys].astype(F32)
        dkv_ref[head] = total
        dq_ref[head] = jnp.zeros(dq_ref.shape[1:], F32)
        for source in range(sources):
            slab = source * rows // LANES * LANES
            piece = part_ref[source, head, :, keys:].astype(F32)
            dq_ref[head, :, slab : slab + LANES] += piece[:head_dim] + piece[head_dim:]


def sum_call(parts, head_dim, rows, queries):
    _, own_heads, _, lanes = parts.shape
    return pl.pallas_call(
        functools.partial(sum_kernel, head_dim=head_dim, rows=rows),
        out_shape=[
            jax.ShapeDtypeStruct((own_heads, 2 * head_dim, lanes - LANES), F32),
            jax.ShapeDtypeStruct((own_heads, head_dim, queries), F32),
        ],
        compiler_params=pltpu.CompilerParams(vmem_limit_bytes=SMALL_LIMIT),
        name="sum_sources",
    )(parts)


def finish_kernel(dkv_ref, dkv_other, dq_ref, dq_other, grad_q, grad_k, grad_v, *, head_dim):
    scale = 1.0 / math.sqrt(head_dim)
    total = dkv_ref[...] + dkv_other[...]
    grad_q[...] = ((dq_ref[...] + dq_other[...]) * scale).astype(BF16)
    grad_k[...] = (total[:, :head_dim, :] * scale).astype(BF16)
    grad_v[...] = total[:, head_dim:, :].astype(BF16)


def finish_call(dkv, dkv_other, dq, dq_other):
    own_heads, head_dim, queries = dq.shape
    keys = dkv.shape[2]
    return pl.pallas_call(
        functools.partial(finish_kernel, head_dim=head_dim),
        out_shape=[
            jax.ShapeDtypeStruct((own_heads, head_dim, queries), BF16),
            jax.ShapeDtypeStruct((own_heads, head_dim, keys), BF16),
            jax.ShapeDtypeStruct((own_heads, head_dim, keys), BF16),
        ],
        compiler_params=pltpu.CompilerParams(vmem_limit_bytes=SMALL_LIMIT),
        name="finish",
    )(dkv, dkv_other, dq, dq_other)


def per_device(
    pair_feats,
    bucket_ids,
    ln_gain,
    w_in,
    b_in,
    w_out,
    bucket_table,
    key_mask,
    q_heads,
    k_heads,
    v_heads,
    out_heads,
    dout_heads,
    log_norm,
):
    axis_size = lax.axis_size("heads")
    own_heads, head_dim, queries = q_heads.shape
    rows = pair_feats.shape[0]
    gain = ln_gain.reshape(1, -1)

    packed = pack_call(k_heads, v_heads, q_heads, dout_heads, out_heads, log_norm, axis_size, rows)
    received = lax.all_to_all(packed, "heads", split_axis=0, concat_axis=0, tiled=True)
    saved, unit_pairs, inv_std, bias_vals = forward_call(
        pair_feats, bucket_ids, gain, w_in, b_in.reshape(1, -1), w_out.T, bucket_table.T
    )
    received = received.reshape((axis_size * own_heads,) + received.shape[2:])
    dscores, parts = attention_call(bias_vals, received, key_mask, head_dim, rows)
    parts = lax.all_to_all(
        parts.reshape((axis_size, own_heads) + parts.shape[1:]), "heads", split_axis=0, concat_axis=0, tiled=True
    )
    grad_pairs = backward_call(unit_pairs, inv_std, dscores, saved, gain, w_in, w_out.T, 0, rows, None)
    parts, grad_pairs = lax.optimization_barrier((parts, grad_pairs))
    dkv_sum, dq_sum = sum_call(parts, head_dim, rows, queries)
    dkv_other = other_sum(dkv_sum, "query")
    dq_other = other_sum(dq_sum, "key")
    grad_q, grad_k, grad_v = finish_call(dkv_sum, dkv_other, dq_sum, dq_other)
    return (grad_pairs, grad_q, grad_k, grad_v)


def solution(mesh):
    def traced(*args):
        with jax.sharding.use_abstract_mesh(mesh.abstract_mesh):
            return jax.shard_map(
                per_device,
                mesh=mesh,
                in_specs=(
                    P(("query", "heads"), None, "key"),
                    P(("query", "heads"), "key"),
                    P(),
                    P(),
                    P(),
                    P(),
                    P(),
                    P("key"),
                    P("heads", None, "query"),
                    P("heads", None, "key"),
                    P("heads", None, "key"),
                    P("heads", None, "query"),
                    P("heads", None, "query"),
                    P("heads", "query"),
                ),
                out_specs=(
                    P(("query", "heads"), None, "key"),
                    P("heads", None, "query"),
                    P("heads", None, "key"),
                    P("heads", None, "key"),
                ),
                check_vma=False,
            )(*args)

    return traced
```

```python
import functools
import math

import jax
import jax.numpy as jnp
from jax import lax
from jax.experimental import pallas as pl
from jax.experimental.pallas import tpu as pltpu
from jax.sharding import PartitionSpec as P

F32 = jnp.float32
BF16 = jnp.bfloat16
RSQRT2 = 1.0 / math.sqrt(2.0)
EXP2_SCALE = -1.0 / math.log(2.0)
EXP2_SHIFT = math.log2(2.0 / math.sqrt(math.pi))
ROWS = 16
LANES = 128
READY = 2
NT = (((1,), (1,)), ((), ()))
FULL_LIMIT = 60 << 20
BIG_LIMIT = 32 << 20
SMALL_LIMIT = 16 << 20


def low(value):
    return jnp.asarray(value, BF16)


def full_spec(array):
    return pl.BlockSpec(array.shape, lambda *_: (0,) * array.ndim)


def divisor(total, largest):
    return math.gcd(total, largest)


def split_low(values, pieces):
    found = []
    for _ in range(pieces):
        piece = values.astype(BF16).astype(F32)
        found.append(piece)
        values = values - piece
    return found


def as_rows(pieces, count):
    rows = lax.broadcasted_iota(jnp.int32, (count, pieces[0].shape[1]), 0)
    block = jnp.zeros(rows.shape, F32)
    for place, piece in enumerate(pieces):
        block = jnp.where(rows == place, piece, block)
    return block.astype(BF16)


def eye(size):
    rows = lax.broadcasted_iota(jnp.int32, (size, size), 0)
    return jnp.where(rows == lax.broadcasted_iota(jnp.int32, (size, size), 1), 1.0, 0.0).astype(BF16)


def transposed(block):
    return lax.dot_general(eye(block.shape[1]), block, NT, preferred_element_type=F32)


def gain_columns(gain_row):
    chans = gain_row.shape[1]
    total = None
    for piece in split_low(gain_row, 3):
        spread = jnp.broadcast_to(piece, (LANES, chans)).astype(BF16)
        part = lax.dot_general(eye(chans), spread, NT, preferred_element_type=F32)
        total = part if total is None else total + part
    return total


def widen(block, tile):
    return jnp.concatenate([block] * (tile // block.shape[1]), axis=1)


def other_sum(values, name):
    if lax.axis_size(name) == 2:
        return lax.ppermute(values, name, [(0, 1), (1, 0)])
    return lax.psum(values, name) - values


def pack_kernel(k_ref, v_ref, q_ref, dout_ref, out_ref, norm_ref, send_ref, *, rows):
    targets, own_heads, depth, lanes = send_ref.shape
    head_dim = k_ref.shape[1]
    keys = lanes - LANES
    half = LANES // 2
    lane = lax.broadcasted_iota(jnp.int32, (depth, LANES), 1)
    for head in range(own_heads):
        dout = dout_ref[head]
        deltas = jnp.sum(dout.astype(F32) * out_ref[head].astype(F32), axis=0, keepdims=True)
        scalars = as_rows(split_low(norm_ref[head : head + 1, :], 3) + split_low(deltas, 3), depth).astype(F32)
        heads_part = jnp.concatenate([q_ref[head], dout], axis=0).astype(F32)
        for target in range(targets):
            send_ref[target, head, :head_dim, :keys] = k_ref[head]
            send_ref[target, head, head_dim:, :keys] = v_ref[head]
            slab = target * rows // LANES * LANES
            window = (lane >= target * rows - slab) & (lane < target * rows - slab + rows)
            turned = [scalars[:, slab + half : slab + LANES], scalars[:, slab : slab + half]]
            extra = jnp.where(window, heads_part[:, slab : slab + LANES], jnp.concatenate(turned, axis=1))
            send_ref[target, head, :, keys:] = extra.astype(BF16)


def pack_call(k_heads, v_heads, q_heads, dout_heads, out_heads, log_norm, targets, rows):
    own_heads, head_dim, keys = k_heads.shape
    return pl.pallas_call(
        functools.partial(pack_kernel, rows=rows),
        out_shape=jax.ShapeDtypeStruct((targets, own_heads, 2 * head_dim, keys + LANES), BF16),
        compiler_params=pltpu.CompilerParams(vmem_limit_bytes=FULL_LIMIT),
        name="pack_heads",
    )(k_heads, v_heads, q_heads, dout_heads, out_heads, log_norm)


def slope_of(scaled, cdf2):
    density2 = jnp.exp2(scaled * scaled * low(EXP2_SCALE) + low(EXP2_SHIFT))
    return cdf2 + scaled * density2


def unit_norm(values):
    centre = values - jnp.mean(values, axis=0, keepdims=True)
    inv_std = lax.rsqrt(jnp.mean(centre * centre, axis=0, keepdims=True) + 1e-05)
    return centre * inv_std, inv_std


def forward_kernel(
    pair_ref, bucket_ref, gain_ref, w_in_ref, b_in_ref, w_out_ref, table_ref, saved_ref, unit_ref, inv_ref, bias_ref, w_pre,
    w_mix, table, gain, *, group, merge, ready
):
    rows, chans, keys = pair_ref.shape
    heads, buckets = table_ref.shape
    width = merge * keys
    first_row = pl.program_id(0) * rows

    @pl.when(pl.program_id(0) == 0)
    def _():
        stacked = jnp.concatenate([w_in_ref[...], as_rows(split_low(b_in_ref[...], 3), ROWS)], axis=0)
        w_pre[...] = transposed(stacked).astype(BF16)
        w_mix[...] = (w_out_ref[...].astype(F32) * 0.5).astype(BF16)
        place = jnp.where(
            lax.broadcasted_iota(jnp.int32, (buckets, LANES), 0) == lax.broadcasted_iota(jnp.int32, (buckets, LANES), 1),
            1.0,
            0.0,
        ).astype(BF16)
        table[...] = jnp.dot(table_ref[...], place, preferred_element_type=F32)
        gain[...] = gain_columns(gain_ref[...])

    def some_rows(row, with_slope):
        pairs = jnp.concatenate([pair_ref[row + member] for member in range(merge)], axis=1)
        unit_pairs, inv_std = unit_norm(pairs.astype(F32))
        unit_low = unit_pairs.astype(BF16)
        normed = (unit_pairs * widen(gain[...], width)).astype(BF16)
        ones = jnp.where(lax.broadcasted_iota(jnp.int32, (ROWS, width), 0) < 3, 1.0, 0.0).astype(BF16)
        pre_act = jnp.dot(w_pre[...], jnp.concatenate([normed, ones], axis=0), preferred_element_type=F32)
        scaled = pre_act * RSQRT2
        cdf2 = lax.erf(scaled) + 1.0
        hidden = (pre_act * cdf2).astype(BF16)
        saved = scaled.astype(BF16)
        if with_slope:
            saved = slope_of(saved, cdf2.astype(BF16))
        outs = []
        mixed = jnp.dot(w_mix[...], hidden, preferred_element_type=F32)
        for member in range(merge):
            pieces = []
            inv_ref[pl.ds(row + member, 1), :] = inv_std[:, member * keys : (member + 1) * keys]
            id_row = bucket_ref[pl.ds(first_row + row + member, 1), :]
            for part in range(keys // LANES):
                begin = member * keys + part * LANES
                saved_ref[row + member, part] = saved[:, begin : begin + LANES]
                unit_ref[row + member, part] = unit_low[:, begin : begin + LANES]
                ids = id_row[:, part * LANES : (part + 1) * LANES]
                lookup = jnp.take_along_axis(table[...], jnp.broadcast_to(ids, (heads, LANES)), axis=1)
                pieces.append(mixed[:, begin : begin + LANES] + lookup)
            outs.append(jnp.concatenate(pieces, axis=1))
        return outs

    def step(index, carry):
        outs = []
        for member in range(0, group, merge):
            outs += some_rows(index * group + member, member < ready)
        size = group * heads
        bias_ref[pl.ds(pl.multiple_of(index * size, size), size), :] = jnp.concatenate(outs, axis=0).astype(BF16)
        return carry

    lax.fori_loop(0, rows // group, step, 0)


def forward_call(pair_feats, bucket_ids, gain, w_in, b_in, w_out, table):
    rows, chans, keys = pair_feats.shape
    heads, hid = w_out.shape
    block = divisor(rows, 8)
    parts = keys // LANES
    return pl.pallas_call(
        functools.partial(forward_kernel, group=block, merge=divisor(block, 2), ready=READY),
        grid=(rows // block,),
        in_specs=[
            pl.BlockSpec((block, chans, keys), lambda i: (i, 0, 0)),
            full_spec(bucket_ids),
            full_spec(gain),
            full_spec(w_in),
            full_spec(b_in),
            full_spec(w_out),
            full_spec(table),
        ],
        out_specs=[
            pl.BlockSpec((block, parts, hid, LANES), lambda i: (i, 0, 0, 0)),
            pl.BlockSpec((block, parts, chans, LANES), lambda i: (i, 0, 0, 0)),
            pl.BlockSpec((block, keys), lambda i: (i, 0)),
            pl.BlockSpec((block * heads, keys), lambda i: (i, 0)),
        ],
        out_shape=[
            jax.ShapeDtypeStruct((rows, parts, hid, LANES), BF16),
            jax.ShapeDtypeStruct((rows, parts, chans, LANES), BF16),
            jax.ShapeDtypeStruct((rows, keys), F32),
            jax.ShapeDtypeStruct((rows * heads, keys), BF16),
        ],
        scratch_shapes=[
            pltpu.VMEM((hid, chans + ROWS), BF16),
            pltpu.VMEM((heads, hid), BF16),
            pltpu.VMEM((heads, LANES), F32),
            pltpu.VMEM((chans, LANES), F32),
        ],
        compiler_params=pltpu.CompilerParams(vmem_limit_bytes=FULL_LIMIT),
        cost_estimate=pl.CostEstimate(
            flops=2 * rows * keys * hid * 256,
            bytes_accessed=2 * rows * keys * (hid + chans),
            transcendentals=2 * rows * keys * hid,
        ),
        name="pair_forward",
    )(pair_feats, bucket_ids, gain, w_in, b_in, w_out, table)


def attention_kernel(
    bias_ref, kv_ref, aux_ref, mask_ref, ds_ref, part_ref, q_rows, d_rows, q_cols, d_cols, norm_ref, delta_ref,
    dq_acc, *, head_dim, rows
):
    heads = kv_ref.shape[0]
    tile = bias_ref.shape[1]
    width = heads * head_dim
    flat = rows * heads
    scale = 1.0 / math.sqrt(head_dim)
    step = pl.program_id(0)
    cols = pl.ds(pl.multiple_of(step * tile, tile), tile)
    offset = lax.rem(lax.axis_index("heads") * rows, LANES)
    scalar_offset = lax.rem(offset + LANES // 2, LANES)

    def spread_matrix():
        lane = lax.broadcasted_iota(jnp.int32, (flat, LANES), 1)
        return lane == lax.broadcasted_iota(jnp.int32, (flat, LANES), 0) // heads + offset

    def own_columns():
        return (
            lax.broadcasted_iota(jnp.int32, (width, flat), 1) % heads
            == lax.broadcasted_iota(jnp.int32, (width, flat), 0) // head_dim
        )

    @pl.when(step == 0)
    def _():
        spread_low = jnp.where(spread_matrix(), 1.0, 0.0).astype(BF16)
        own_rows = (
            lax.broadcasted_iota(jnp.int32, (flat, width), 0) % heads
            == lax.broadcasted_iota(jnp.int32, (flat, width), 1) // head_dim
        )
        own_cols = own_columns()
        for begin, by_rows, by_cols in ((0, q_rows, q_cols), (head_dim, d_rows, d_cols)):
            block = aux_ref[:, begin : begin + head_dim, :].reshape(width, LANES)
            spread = lax.dot_general(spread_low, block, NT, preferred_element_type=F32)
            by_rows[...] = jnp.where(own_rows, spread, 0.0).astype(BF16)
            spread = lax.dot_general(block, spread_low, NT, preferred_element_type=F32)
            by_cols[...] = jnp.where(own_cols, spread, 0.0).astype(BF16)
        tail = aux_ref[:, :ROWS, :].astype(F32)
        lane = lax.broadcasted_iota(jnp.int32, (rows, heads, LANES), 2)
        own_lane = lane == lax.broadcasted_iota(jnp.int32, (rows, heads, LANES), 0) + scalar_offset
        for begin, target in ((0, norm_ref), (3, delta_ref)):
            pieces = tail[:, begin, :] + tail[:, begin + 1, :] + tail[:, begin + 2, :]
            column = jnp.sum(jnp.where(own_lane, pieces[None], 0.0), axis=2, keepdims=True)
            target[...] = jnp.broadcast_to(column.reshape(flat, 1), target.shape)
        dq_acc[...] = jnp.zeros_like(dq_acc)

    norm = widen(norm_ref[...], tile)
    delta = widen(delta_ref[...], tile)
    keys = kv_ref[:, :head_dim, :].reshape(width, tile)
    values = kv_ref[:, head_dim:, :].reshape(width, tile)
    scores = jnp.dot(q_rows[...], keys, preferred_element_type=F32) * scale + bias_ref[...].astype(F32)
    probs = jnp.where(mask_ref[...] == 1, jnp.exp(scores - norm), 0.0)
    dprobs = jnp.dot(d_rows[...], values, preferred_element_type=F32)
    dscores = (probs * (dprobs - delta)).astype(BF16)
    ds_ref[...] = dscores
    dk_part = jnp.dot(q_cols[...], dscores, preferred_element_type=F32)
    dv_part = jnp.dot(d_cols[...], probs.astype(BF16), preferred_element_type=F32)
    part_ref[:, :head_dim, cols] = dk_part.reshape(heads, head_dim, tile).astype(BF16)
    part_ref[:, head_dim : 2 * head_dim, cols] = dv_part.reshape(heads, head_dim, tile).astype(BF16)
    dq_acc[...] += lax.dot_general(keys, dscores, NT, preferred_element_type=F32)

    @pl.when(step == pl.num_programs(0) - 1)
    def _():
        spread_low = jnp.where(spread_matrix(), 1.0, 0.0).astype(BF16)
        total = None
        for piece in split_low(jnp.where(own_columns(), dq_acc[...], 0.0), 3):
            part = jnp.dot(piece.astype(BF16), spread_low, preferred_element_type=F32)
            total = part if total is None else total + part
        high, rest = split_low(total, 2)
        keys_end = part_ref.shape[2] - LANES
        part_ref[:, :head_dim, keys_end:] = high.astype(BF16).reshape(heads, head_dim, LANES)
        part_ref[:, head_dim:, keys_end:] = rest.astype(BF16).reshape(heads, head_dim, LANES)


def attention_call(bias, received, key_mask, head_dim, rows):
    flat, keys = bias.shape
    heads, depth, _ = received.shape
    width = heads * head_dim
    tile = divisor(keys, 1024)
    return pl.pallas_call(
        functools.partial(attention_kernel, head_dim=head_dim, rows=rows),
        grid=(keys // tile,),
        in_specs=[
            pl.BlockSpec((flat, tile), lambda i: (0, i)),
            pl.BlockSpec((heads, 2 * head_dim, tile), lambda i: (0, 0, i)),
            pl.BlockSpec((heads, depth, LANES), lambda i: (0, 0, keys // LANES)),
            pl.BlockSpec((1, tile), lambda i: (0, i)),
        ],
        out_specs=[
            pl.BlockSpec((flat, tile), lambda i: (0, i)),
            pl.BlockSpec((heads, depth, keys + LANES), lambda i: (0, 0, 0)),
        ],
        out_shape=[
            pltpu.HBM((flat, keys), BF16),
            jax.ShapeDtypeStruct((heads, depth, keys + LANES), BF16),
        ],
        scratch_shapes=[
            pltpu.VMEM((flat, width), BF16),
            pltpu.VMEM((flat, width), BF16),
            pltpu.VMEM((width, flat), BF16),
            pltpu.VMEM((width, flat), BF16),
            pltpu.VMEM((flat, LANES), F32),
            pltpu.VMEM((flat, LANES), F32),
            pltpu.VMEM((width, flat), F32),
        ],
        compiler_params=pltpu.CompilerParams(vmem_limit_bytes=BIG_LIMIT),
        cost_estimate=pl.CostEstimate(
            flops=10 * flat * keys * width, bytes_accessed=8 * flat * keys, transcendentals=flat * keys
        ),
        name="pair_attention",
    )(pltpu.with_memory_space_constraint(bias, pltpu.HBM), received, received, key_mask.reshape(1, keys))


def backward_kernel(unit_ref, inv_ref, ds_ref, saved_ref, gain_ref, w_in_ref, w_out_ref, *rest, group, merge, ready):
    out_ref, w_back, gain = rest[-3:]
    rows, parts, chans, _ = unit_ref.shape
    heads = w_out_ref.shape[0]
    keys = parts * LANES

    @pl.when(pl.program_id(0) == 0)
    def _():
        w_back[...] = (transposed(w_out_ref[...]) * 0.5).astype(BF16)
        gain[...] = gain_columns(gain_ref[...])

    def step(index, carry):
        size = group * heads
        dscores = ds_ref[pl.ds(pl.multiple_of(index * size, size), size), :]
        for begin in range(0, group, merge):
            members = range(begin, begin + merge)
            tiles = [(index * group + member, part) for member in members for part in range(parts)]
            unit_pairs = jnp.concatenate([unit_ref[row, part] for row, part in tiles], axis=1).astype(F32)
            saved = jnp.concatenate([saved_ref[row, part] for row, part in tiles], axis=1)
            inv_std = jnp.concatenate([inv_ref[pl.ds(index * group + member, 1), :] for member in members], axis=1)
            own = [dscores[member * heads : (member + 1) * heads] for member in members]
            slope = saved if begin < ready else slope_of(saved, lax.erf(saved) + low(1.0))
            dhidden = jnp.dot(w_back[...], jnp.concatenate(own, axis=1), preferred_element_type=F32)
            dpre = dhidden.astype(BF16) * slope
            dunit = jnp.dot(w_in_ref[...], dpre, preferred_element_type=F32) * widen(gain[...], keys * merge)
            first_mean = jnp.mean(dunit, axis=0, keepdims=True)
            second_mean = jnp.mean(dunit * unit_pairs, axis=0, keepdims=True)
            grad = (inv_std * (dunit - first_mean - unit_pairs * second_mean)).astype(BF16)
            for place, member in enumerate(members):
                out_ref[index * group + member] = grad[:, place * keys : (place + 1) * keys]
        return carry

    lax.fori_loop(0, rows // group, step, 0)


def backward_call(unit_pairs, inv_std, dscores, saved, gain, w_in, w_out, begin, count, previous):
    rows, parts, chans, _ = unit_pairs.shape
    keys = parts * LANES
    heads, hid = w_out.shape
    block = divisor(math.gcd(begin, count), 8)
    first = begin // block
    operands = [unit_pairs, inv_std, dscores, saved, gain, w_in, w_out]
    in_specs = [
        pl.BlockSpec((block, parts, chans, LANES), lambda i: (i + first, 0, 0, 0)),
        pl.BlockSpec((block, keys), lambda i: (i + first, 0)),
        pl.BlockSpec((block * heads, keys), lambda i: (i + first, 0)),
        pl.BlockSpec((block, parts, hid, LANES), lambda i: (i + first, 0, 0, 0)),
        full_spec(gain),
        full_spec(w_in),
        full_spec(w_out),
    ]
    aliases = {}
    if previous is not None:
        aliases = {len(operands): 0}
        operands.append(previous)
        in_specs.append(pl.BlockSpec(memory_space=pl.ANY))
    return pl.pallas_call(
        functools.partial(backward_kernel, group=block, merge=divisor(block, 2), ready=READY),
        grid=(count // block,),
        in_specs=in_specs,
        out_specs=pl.BlockSpec((block, chans, keys), lambda i: (i + first, 0, 0)),
        out_shape=jax.ShapeDtypeStruct((rows, chans, keys), BF16),
        scratch_shapes=[pltpu.VMEM((hid, heads), BF16), pltpu.VMEM((chans, LANES), F32)],
        input_output_aliases=aliases,
        compiler_params=pltpu.CompilerParams(vmem_limit_bytes=FULL_LIMIT),
        cost_estimate=pl.CostEstimate(
            flops=2 * count * keys * hid * 256,
            bytes_accessed=2 * count * keys * (hid + 2 * chans),
            transcendentals=0,
        ),
        name="pair_backward",
    )(*operands)


def sum_kernel(part_ref, dkv_ref, dq_ref, *, head_dim, rows):
    sources, own_heads, _, lanes = part_ref.shape
    keys = lanes - LANES
    for head in range(own_heads):
        total = part_ref[0, head, :, :keys].astype(F32)
        for source in range(1, sources):
            total = total + part_ref[source, head, :, :keys].astype(F32)
        dkv_ref[head] = total
        dq_ref[head] = jnp.zeros(dq_ref.shape[1:], F32)
        for source in range(sources):
            slab = source * rows // LANES * LANES
            piece = part_ref[source, head, :, keys:].astype(F32)
            dq_ref[head, :, slab : slab + LANES] += piece[:head_dim] + piece[head_dim:]


def sum_call(parts, head_dim, rows, queries):
    _, own_heads, _, lanes = parts.shape
    return pl.pallas_call(
        functools.partial(sum_kernel, head_dim=head_dim, rows=rows),
        out_shape=[
            jax.ShapeDtypeStruct((own_heads, 2 * head_dim, lanes - LANES), F32),
            jax.ShapeDtypeStruct((own_heads, head_dim, queries), F32),
        ],
        compiler_params=pltpu.CompilerParams(vmem_limit_bytes=SMALL_LIMIT),
        name="sum_sources",
    )(parts)


def finish_kernel(dkv_ref, dkv_other, dq_ref, dq_other, grad_q, grad_k, grad_v, *, head_dim):
    scale = 1.0 / math.sqrt(head_dim)
    total = dkv_ref[...] + dkv_other[...]
    grad_q[...] = ((dq_ref[...] + dq_other[...]) * scale).astype(BF16)
    grad_k[...] = (total[:, :head_dim, :] * scale).astype(BF16)
    grad_v[...] = total[:, head_dim:, :].astype(BF16)


def finish_call(dkv, dkv_other, dq, dq_other):
    own_heads, head_dim, queries = dq.shape
    keys = dkv.shape[2]
    return pl.pallas_call(
        functools.partial(finish_kernel, head_dim=head_dim),
        out_shape=[
            jax.ShapeDtypeStruct((own_heads, head_dim, queries), BF16),
            jax.ShapeDtypeStruct((own_heads, head_dim, keys), BF16),
            jax.ShapeDtypeStruct((own_heads, head_dim, keys), BF16),
        ],
        compiler_params=pltpu.CompilerParams(vmem_limit_bytes=SMALL_LIMIT),
        name="finish",
    )(dkv, dkv_other, dq, dq_other)


def per_device(
    pair_feats,
    bucket_ids,
    ln_gain,
    w_in,
    b_in,
    w_out,
    bucket_table,
    key_mask,
    q_heads,
    k_heads,
    v_heads,
    out_heads,
    dout_heads,
    log_norm,
):
    axis_size = lax.axis_size("heads")
    own_heads, head_dim, queries = q_heads.shape
    rows = pair_feats.shape[0]
    gain = ln_gain.reshape(1, -1)

    packed = pack_call(k_heads, v_heads, q_heads, dout_heads, out_heads, log_norm, axis_size, rows)
    received = lax.all_to_all(packed, "heads", split_axis=0, concat_axis=0, tiled=True)
    saved, unit_pairs, inv_std, bias_vals = forward_call(
        pair_feats, bucket_ids, gain, w_in, b_in.reshape(1, -1), w_out.T, bucket_table.T
    )
    received = received.reshape((axis_size * own_heads,) + received.shape[2:])
    dscores, parts = attention_call(bias_vals, received, key_mask, head_dim, rows)
    parts = lax.all_to_all(
        parts.reshape((axis_size, own_heads) + parts.shape[1:]), "heads", split_axis=0, concat_axis=0, tiled=True
    )
    grad_pairs = backward_call(unit_pairs, inv_std, dscores, saved, gain, w_in, w_out.T, 0, rows, None)
    parts, grad_pairs = lax.optimization_barrier((parts, grad_pairs))
    dkv_sum, dq_sum = sum_call(parts, head_dim, rows, queries)
    dq_other = other_sum(dq_sum, "key")
    dkv_other = other_sum(dkv_sum, "query")
    grad_q, grad_k, grad_v = finish_call(dkv_sum, dkv_other, dq_sum, dq_other)
    return (grad_pairs, grad_q, grad_k, grad_v)


def solution(mesh):
    def traced(*args):
        with jax.sharding.use_abstract_mesh(mesh.abstract_mesh):
            return jax.shard_map(
                per_device,
                mesh=mesh,
                in_specs=(
                    P(("query", "heads"), None, "key"),
                    P(("query", "heads"), "key"),
                    P(),
                    P(),
                    P(),
                    P(),
                    P(),
                    P("key"),
                    P("heads", None, "query"),
                    P("heads", None, "key"),
                    P("heads", None, "key"),
                    P("heads", None, "query"),
                    P("heads", None, "query"),
                    P("heads", "query"),
                ),
                out_specs=(
                    P(("query", "heads"), None, "key"),
                    P("heads", None, "query"),
                    P("heads", None, "key"),
                    P("heads", None, "key"),
                ),
                check_vma=False,
            )(*args)

    return traced
```
